768 devices in a mesh: mom: 24 (over z_hi, y), trow: 4 (over z_lo), tcol: 8 (over x, core).
Axes of the slice: x: 4, y: 8, z: 12 (z_hi: 3, z_lo: 4; z = z_hi * 4 + z_lo), core: 2. Of those that a mesh axis runs over, the one named last changes fastest.
Arguments:
- g_free: float32 [2, 24, 1536, 1536], P(None, 'mom', 'tcol', 'trow'), may hold values from -6 to 6
- g_greater_t: float32 [2, 24, 1536, 1536], P(None, 'mom', 'tcol', 'trow'), may hold values from -6 to 6
- momentum_map: int32 [24], replicated, may hold values from 0 to 23, each once
- weights: float32 [1536], replicated, may hold values from 0.00076546555 to 0.0076546553
Outputs:
- g_out: float32 [2, 24, 1536, 1536], P(None, 'mom', 'tcol', 'trow')
The draws below stay inside these ranges and needn't reach their ends.
Inputs may be any that keep to these rules, and one draw needn't show every extreme that they name: `momentum_map`: each number appears once.
All inputs are finite; a program needn't handle non-finite values.
Results may differ from the reference program's by a relative error of at most 0.00022.
Values sent between devices are 32-bit elements; how exact they have to be, the bound alone decides.
No kernel may reach another device: no remote copies, remote signals or barrier semaphores. Data moves between devices by JAX's collectives and lax.ppermute only.
A program may use at most 32 MiB of HBM per device.

```python
import math
import jax
import jax.numpy as jnp
from jax import lax

LY = 4
K = 24
NT = 1536
ITERS = 2


def block_levels(rng, dims, cuts, smallest, high):
    gain = 1.0
    for dim, parts in cuts:
        draws = jax.random.uniform(jax.random.fold_in(jax.random.fold_in(rng, 6), dim), (parts,), jnp.float32, smallest / len(cuts), high / len(cuts))
        gain = gain * jnp.repeat(jnp.exp(draws), dims[dim] // parts).reshape((-1,) + (1,) * (len(dims) - 1 - dim))
    return gain


def scatter_about(stream_key, dims, width, most, cuts=(), held_as=jnp.bfloat16):
    level = block_levels(stream_key, dims, cuts, -0.22, 0.18) if cuts else 1.0
    values = jax.random.normal(stream_key, dims, jnp.float32) * width * level
    return jnp.minimum(jnp.maximum(values, -most), most).astype(held_as)


def setup_inputs(seed: int = 0) -> dict:
    streams_of = jax.random.split(jax.random.key(seed), 5)
    g_free = scatter_about(streams_of[0], (2, K, NT, NT), 1.0, 6.0, ((1, 24), (2, 8), (3, 4)), jnp.float32)
    g_greater_t = scatter_about(streams_of[1], (2, K, NT, NT), 1.0, 6.0, ((1, 24), (2, 8), (3, 4)), jnp.float32)
    momentum_map = jax.random.permutation(streams_of[2], K).astype(jnp.int32)
    weights = jnp.clip(jnp.exp(jax.random.uniform(streams_of[3], (NT,), jnp.float32, math.log(0.00076546555), math.log(0.0076546553))), 0.00076546555, 0.0076546553)
    return dict(g_free=g_free, g_greater_t=g_greater_t, momentum_map=momentum_map, weights=weights)


highest = lax.Precision.HIGHEST

def matmul(left_side, right_side):
    return jnp.dot(left_side, right_side, precision=highest, preferred_element_type=jnp.float32)

def phase_tables(momentum_map):
    momenta = momentum_map.shape[0]
    across = momenta // LY
    site_index = jnp.arange(momenta, dtype=jnp.int32)
    wave_x = momentum_map % across
    wave_y = momentum_map // across
    site_x = site_index % across
    site_y = site_index // across
    phase_turns = site_x[:, None] * wave_x[None, :] % across * LY + site_y[:, None] * wave_y[None, :] % LY * across
    angles = phase_turns.astype(jnp.float32) * (2.0 * math.pi / momenta)
    norm_scale = 1.0 / math.sqrt(momenta)
    return (jnp.cos(angles) * norm_scale, jnp.sin(angles) * norm_scale)

def mirrored(cosine_table, sine_table, real_part, imag_part):
    return (matmul(cosine_table, real_part) + matmul(sine_table, imag_part), matmul(cosine_table, imag_part) - matmul(sine_table, real_part))

def self_energy(cosine_table, sine_table, lesser_real, lesser_imag, mirror_real, mirror_imag):
    space_real = matmul(cosine_table, lesser_real) - matmul(sine_table, lesser_imag)
    space_imag = matmul(sine_table, lesser_real) + matmul(cosine_table, lesser_imag)
    square_real = space_real * space_real - space_imag * space_imag
    square_imag = 2.0 * space_real * space_imag
    source_real = square_real * mirror_real - square_imag * mirror_imag
    source_imag = square_real * mirror_imag + square_imag * mirror_real
    sigma_real = matmul(cosine_table.T, source_real) + matmul(sine_table.T, source_imag)
    sigma_imag = matmul(cosine_table.T, source_imag) - matmul(sine_table.T, source_real)
    return jnp.stack([sigma_real, sigma_imag])

def contract(left_side, right_side):
    return jnp.einsum('krs,ksc->krc', left_side, right_side, precision=highest, preferred_element_type=jnp.float32)

def weighted_product(sigma_part, green_part):
    real_part = contract(sigma_part[0], green_part[0]) - contract(sigma_part[1], green_part[1])
    imag_part = contract(sigma_part[0], green_part[1]) + contract(sigma_part[1], green_part[0])
    return jnp.stack([real_part, imag_part])

def reference(g_free, g_greater_t, momentum_map, weights):
    cosine_table, sine_table = phase_tables(momentum_map)
    cells = NT * NT
    greater_flat = g_greater_t.reshape(2, K, cells)
    mirror_real, mirror_imag = mirrored(cosine_table, sine_table, greater_flat[0], greater_flat[1])
    green_now = g_free
    for sweep in range(ITERS):
        flat = green_now.reshape(2, K, cells)
        sigma_full = self_energy(cosine_table, sine_table, flat[0], flat[1], mirror_real, mirror_imag).reshape(2, K, NT, NT)
        sigma_weighted = sigma_full * weights

        def one_momentum(pair):
            return weighted_product(pair[0][:, None], pair[1][:, None])[:, 0]
        correction = lax.map(one_momentum, (jnp.moveaxis(sigma_weighted, 1, 0), jnp.moveaxis(green_now, 1, 0)))
        green_now = g_free + jnp.moveaxis(correction, 0, 1)
    return green_now
```

```python
import math

import jax
import jax.numpy as jnp
from jax import lax
from jax.experimental import pallas as pl
from jax.experimental.pallas import tpu as pltpu
from jax.sharding import Mesh, PartitionSpec as P

LY = 4
ITERS = 2


LANES = 128
ROOT3_2 = math.sqrt(3.0) / 2.0


def c_add(a, b):
    return (a[0] + b[0], a[1] + b[1])


def c_sub(a, b):
    return (a[0] - b[0], a[1] - b[1])


def c_turn(a, sign):
    return (-a[1], a[0]) if sign > 0 else (a[1], -a[0])


def dft3(x0, x1, x2, sign):
    u = c_add(x1, x2)
    v = c_sub(x1, x2)
    m = (x0[0] - 0.5 * u[0], x0[1] - 0.5 * u[1])
    n = c_turn((ROOT3_2 * v[0], ROOT3_2 * v[1]), sign)
    return c_add(x0, u), c_add(m, n), c_sub(m, n)


def dft4(x, sign):
    t0, t1 = c_add(x[0], x[2]), c_sub(x[0], x[2])
    t2, t3 = c_add(x[1], x[3]), c_turn(c_sub(x[1], x[3]), sign)
    return [c_add(t0, t2), c_add(t1, t3), c_sub(t0, t2), c_sub(t1, t3)]


def dft6(x, sign):
    b = [c_add(x[m], x[m + 3]) for m in range(3)]
    c = [c_sub(x[m], x[m + 3]) for m in range(3)]
    even = dft3(b[0], b[1], b[2], sign)
    odd = dft3(c[0], (-c[1][0], -c[1][1]), c[2], sign)
    return [even[0], odd[2], even[1], odd[0], even[2], odd[1]]


def lattice_transform(x, sign):
    rows = [[None] * 6 for _ in range(4)]
    for across in range(6):
        column = dft4([x[6 * down + across] for down in range(4)], sign)
        for down in range(4):
            rows[down][across] = column[down]
    out = []
    for down in range(4):
        out.extend(dft6(rows[down], sign))
    return out


def self_energy_kernel(first, map_ref, weights_ref, field_ref, *refs):
    if first:
        sigma_ref, mirror_ref, where_ref = refs
    else:
        mirror_ref, sigma_ref, where_ref = refs
    momenta = field_ref.shape[0]
    for k in range(momenta):
        where_ref[map_ref[k]] = k
    spot = [where_ref[q] for q in range(momenta)]
    zl = lax.axis_index("zl")
    for lane in range(0, field_ref.shape[3], LANES):
        cut = pl.ds(lane, LANES)
        if first:
            mirror = lattice_transform(
                [(field_ref[k, 2, :, cut], field_ref[k, 3, :, cut]) for k in spot], -1
            )
            scale = 1.0 / (momenta * momenta)
            for r in range(momenta):
                mirror_ref[r, 0, :, cut] = mirror[r][0] * scale
                mirror_ref[r, 1, :, cut] = mirror[r][1] * scale
        space = lattice_transform(
            [(field_ref[k, 0, :, cut], field_ref[k, 1, :, cut]) for k in spot], 1
        )
        source = []
        for r in range(momenta):
            re, im = space[r]
            sq_re = re * re - im * im
            sq_im = 2.0 * re * im
            m_re, m_im = mirror_ref[r, 0, :, cut], mirror_ref[r, 1, :, cut]
            source.append((sq_re * m_re - sq_im * m_im, sq_re * m_im + sq_im * m_re))
        sigma = lattice_transform(source, -1)
        w = weights_ref[zl, :, cut]
        for q in range(momenta):
            sigma_ref[spot[q], 0, :, cut] = sigma[q][0] * w
            sigma_ref[spot[q], 1, :, cut] = sigma[q][1] * w


def self_energy(momentum_map, weights, field, mirror=None):
    first = mirror is None
    momenta, _, rows, cols = field.shape
    shape = jax.ShapeDtypeStruct((momenta, 2, rows, cols), jnp.float32)
    smem = pl.BlockSpec(memory_space=pltpu.SMEM)
    vmem = pl.BlockSpec(memory_space=pltpu.VMEM)
    ins = [momentum_map, weights, field] + ([] if first else [mirror])
    return pl.pallas_call(
        lambda *refs: self_energy_kernel(first, *refs),
        out_shape=(shape, shape) if first else shape,
        in_specs=[smem] + [vmem] * (len(ins) - 1),
        out_specs=(vmem, vmem) if first else vmem,
        scratch_shapes=[pltpu.SMEM((momenta,), jnp.int32)],
        name="self_energy_first" if first else "self_energy_next",
    )(*ins)


def split_left(x):
    hi = x.astype(jnp.bfloat16)
    lo = (x - hi.astype(jnp.float32)).astype(jnp.bfloat16)
    return jnp.concatenate([hi, lo, hi], axis=1)


def split_right(x):
    hi = x.astype(jnp.bfloat16)
    lo = (x - hi.astype(jnp.float32)).astype(jnp.bfloat16)
    return jnp.concatenate([hi, hi, lo], axis=0)


def product_kernel(n_left, blocks, n_out, panel_fmt, zl_ref, *refs):
    lefts, refs = refs[:n_left], refs[n_left:]
    panel_ref, base_ref, refs = refs[0], refs[1], refs[2:]
    out_refs = refs
    groups, _, rows, cols = lefts[0].shape

    def part(j):
        total = lefts[0][:, j]
        for ref in lefts[1:]:
            total = total + ref[:, j]
        return total.reshape(groups * rows, cols)

    def right(j):
        x = panel_ref[:, j]
        return x.reshape(x.shape[0] * x.shape[1], x.shape[2])

    s_re, s_im = part(0), part(1)
    g_re, g_im = right(0), right(1)

    def mul(a, b):
        return jnp.dot(split_left(a), split_right(b), preferred_element_type=jnp.float32)

    one = mul(s_re, g_re)
    two = mul(s_im, g_im)
    three = mul(s_re + s_im, g_re + g_im)
    res = (base_ref[0] + (one - two), base_ref[1] + (three - one - two))
    out_refs[0][0] = res[0]
    out_refs[0][1] = res[1]
    if n_out == 2:
        out_refs[1][:, 0] = res[0].reshape(groups, rows, cols)
        out_refs[1][:, 1] = res[1].reshape(groups, rows, cols)


def product(lefts, panel, block, base, tiled_out=False):
    groups, _, rows, cols = lefts[0].shape
    tile = base.shape
    n_parts = panel.shape[0] * tile[1] // cols
    per = panel.shape[0] // n_parts
    full = lambda shape: pl.BlockSpec(shape, lambda i, b: (0,) * len(shape))
    outs = [jax.ShapeDtypeStruct(tile, jnp.float32)]
    if tiled_out:
        outs.append(jax.ShapeDtypeStruct(lefts[0].shape, jnp.float32))
    res = pl.pallas_call(
        lambda *refs: product_kernel(len(lefts), None, len(outs), None, *refs),
        out_shape=outs,
        grid_spec=pltpu.PrefetchScalarGridSpec(
            num_scalar_prefetch=1,
            grid=(1,),
            in_specs=[full(x.shape) for x in lefts]
            + [
                pl.BlockSpec((per,) + panel.shape[1:], lambda i, b: (b[0], 0, 0, 0)),
                full(tile),
            ],
            out_specs=[full(o.shape) for o in outs],
        ),
        name="product_tiled" if tiled_out else "product",
    )(block.reshape(1), *lefts, panel, base)
    return res if tiled_out else res[0]


def time_product(sigma, panel, base, tiled_out):
    zl = lax.axis_index("zl")
    low = zl < 2
    near = lax.ppermute(sigma, "zl", [(0, 1), (1, 0), (2, 3), (3, 2)])
    mid = lax.ppermute(sigma, "zl", [(1, 2), (2, 1)])
    total = product([sigma], panel, zl, base)
    end_two = lax.ppermute(mid, "zl", [(1, 0), (2, 3)])
    mid_far = lax.ppermute(near, "zl", [(1, 2), (2, 1)])
    total = product([near], panel, lax.bitwise_xor(zl, 1), total)
    end_far = lax.ppermute(mid_far, "zl", [(1, 0), (2, 3)])
    total = product([mid, end_two], panel, jnp.where(low, 2, 1), total)
    return product([mid_far, end_far], panel, jnp.where(low, 3, 0), total, tiled_out)


def body(g_free, g_greater_t, momentum_map, weights):
    momenta = momentum_map.shape[0]
    tile_rows, tile_cols = g_free.shape[2], g_free.shape[3]
    rows = tile_rows // momenta
    free = g_free[:, 0]
    weights = weights.reshape(-1, 1, tile_cols)

    panel = lax.all_gather(free, ("x", "core"))
    both = jnp.concatenate([free, g_greater_t[:, 0]], axis=0)
    both = both.reshape(4, momenta, rows, tile_cols).swapaxes(0, 1)
    field = lax.all_to_all(both, ("zh", "y"), 0, 0, tiled=True)
    sigma, mirror = self_energy(momentum_map, weights, field)
    for sweep in range(ITERS):
        sigma = lax.all_to_all(sigma, ("zh", "y"), 0, 0, tiled=True)
        if sweep == ITERS - 1:
            return time_product(sigma, panel, free, False)[:, None]
        green, tiled = time_product(sigma, panel, free, True)
        panel = lax.all_gather(green, ("x", "core"))
        field = lax.all_to_all(tiled, ("zh", "y"), 0, 0, tiled=True)
        sigma = self_energy(momentum_map, weights, field, mirror)


def solution(mesh):
    fine = Mesh(mesh.devices.reshape(3, 8, 4, 4, 2), ("zh", "y", "zl", "x", "core"))
    spec = P(None, ("zh", "y"), ("x", "core"), "zl")
    return jax.shard_map(
        body, mesh=fine, in_specs=(spec, spec, P(), P()), out_specs=spec, check_vma=False
    )
```

```python
import math

import jax
import jax.numpy as jnp
from jax import lax
from jax.experimental import pallas as pl
from jax.experimental.pallas import tpu as pltpu
from jax.sharding import Mesh, PartitionSpec as P

LY = 4
ITERS = 2


CHUNKS = (128, 64)
VMEM = 24 * 1024 * 1024

LANES = 128
SUBLANES = 8
ROOT3_2 = math.sqrt(3.0) / 2.0


def c_add(a, b):
    return (a[0] + b[0], a[1] + b[1])


def c_sub(a, b):
    return (a[0] - b[0], a[1] - b[1])


def c_turn(a, sign):
    return (-a[1], a[0]) if sign > 0 else (a[1], -a[0])


def dft3(x0, x1, x2, sign):
    u = c_add(x1, x2)
    v = c_sub(x1, x2)
    m = (x0[0] - 0.5 * u[0], x0[1] - 0.5 * u[1])
    n = c_turn((ROOT3_2 * v[0], ROOT3_2 * v[1]), sign)
    return c_add(x0, u), c_add(m, n), c_sub(m, n)


def dft4(x, sign):
    t0, t1 = c_add(x[0], x[2]), c_sub(x[0], x[2])
    t2, t3 = c_add(x[1], x[3]), c_turn(c_sub(x[1], x[3]), sign)
    return [c_add(t0, t2), c_add(t1, t3), c_sub(t0, t2), c_sub(t1, t3)]


def dft6(x, sign):
    b = [c_add(x[m], x[m + 3]) for m in range(3)]
    c = [c_sub(x[m], x[m + 3]) for m in range(3)]
    even = dft3(b[0], b[1], b[2], sign)
    odd = dft3(c[0], (-c[1][0], -c[1][1]), c[2], sign)
    return [even[0], odd[2], even[1], odd[0], even[2], odd[1]]


def lattice_transform(x, sign):
    rows = [[None] * 6 for _ in range(4)]
    for across in range(6):
        column = dft4([x[6 * down + across] for down in range(4)], sign)
        for down in range(4):
            rows[down][across] = column[down]
    out = []
    for down in range(4):
        out.extend(dft6(rows[down], sign))
    return out


def self_energy_kernel(first, map_ref, weights_ref, field_ref, *refs):
    if first:
        sigma_ref, mirror_ref, where_ref = refs
    else:
        mirror_ref, sigma_ref, where_ref = refs
    momenta = field_ref.shape[0]
    for k in range(momenta):
        where_ref[map_ref[k]] = k
    spot = [where_ref[q] for q in range(momenta)]
    slab = lax.axis_index("zh") * lax.axis_size("y") + lax.axis_index("y")
    per_tile = weights_ref.shape[0] // lax.axis_size("zl")
    w = weights_ref[lax.axis_index("zl") * per_tile + lax.rem(slab, per_tile)]
    for row in range(0, field_ref.shape[2], SUBLANES):
        cut = pl.ds(row, SUBLANES)
        if first:
            mirror = lattice_transform(
                [(field_ref[k, 2, cut], field_ref[k, 3, cut]) for k in spot], -1
            )
            scale = 1.0 / (momenta * momenta)
            for r in range(momenta):
                mirror_ref[r, 0, cut] = mirror[r][0] * scale
                mirror_ref[r, 1, cut] = mirror[r][1] * scale
        space = lattice_transform([(field_ref[k, 0, cut], field_ref[k, 1, cut]) for k in spot], 1)
        source = []
        for r in range(momenta):
            re, im = space[r]
            sq_re = re * re - im * im
            sq_im = 2.0 * re * im
            m_re, m_im = mirror_ref[r, 0, cut], mirror_ref[r, 1, cut]
            source.append((sq_re * m_re - sq_im * m_im, sq_re * m_im + sq_im * m_re))
        sigma = lattice_transform(source, -1)
        for q in range(momenta):
            sigma_ref[spot[q], 0, cut] = sigma[q][0] * w
            sigma_ref[spot[q], 1, cut] = sigma[q][1] * w


def self_energy(momentum_map, weights, field, mirror=None):
    first = mirror is None
    momenta, _, rows, cols = field.shape
    shape = jax.ShapeDtypeStruct((momenta, 2, rows, cols), jnp.float32)
    smem = pl.BlockSpec(memory_space=pltpu.SMEM)
    vmem = pl.BlockSpec(memory_space=pltpu.VMEM)
    ins = [momentum_map, weights, field] + ([] if first else [mirror])
    return pl.pallas_call(
        lambda *refs: self_energy_kernel(first, *refs),
        out_shape=(shape, shape) if first else shape,
        in_specs=[smem] + [vmem] * (len(ins) - 1),
        out_specs=(vmem, vmem) if first else vmem,
        scratch_shapes=[pltpu.SMEM((momenta,), jnp.int32)],
        compiler_params=pltpu.CompilerParams(vmem_limit_bytes=VMEM),
        name="self_energy_first" if first else "self_energy_next",
    )(*ins)


def split_left(x):
    hi = x.astype(jnp.bfloat16)
    lo = (x - hi.astype(jnp.float32)).astype(jnp.bfloat16)
    return jnp.concatenate([hi, lo, hi], axis=1)


def split_right(x):
    hi = x.astype(jnp.bfloat16)
    lo = (x - hi.astype(jnp.float32)).astype(jnp.bfloat16)
    return jnp.concatenate([hi, hi, lo], axis=0)


def mul(a, b):
    return jnp.dot(split_left(a), split_right(b), preferred_element_type=jnp.float32)


def product_kernel(n_terms, across, tiled, skip, blocks_ref, *refs):
    terms = []
    for n_left in n_terms:
        terms.append((refs[:n_left], refs[n_left]))
        refs = refs[n_left + 1 :]
    base_ref, refs = refs[0], refs[2 if skip else 1 :]
    out_ref = refs[0]

    def left(holders, j):
        bands = []
        for g in range(0, holders[0].shape[0], across):
            row = []
            for c in range(across):
                piece = holders[0][g + c, j]
                for ref in holders[1:]:
                    piece = piece + ref[g + c, j]
                row.append(piece)
            bands.append(jnp.concatenate(row, axis=1))
        return jnp.concatenate(bands, axis=0)

    def right(ref, j):
        x = ref[:, j]
        return x.reshape(x.shape[0] * x.shape[1], x.shape[2])

    re, im = base_ref[0], base_ref[1]
    for holders, panel_ref in terms:
        s_re, s_im = left(holders, 0), left(holders, 1)
        g_re, g_im = right(panel_ref, 0), right(panel_ref, 1)
        one = mul(s_re, g_re)
        two = mul(s_im, g_im)
        three = mul(s_re + s_im, g_re + g_im)
        re, im = re + (one - two), im + (three - one - two)
    out_ref[0] = re
    out_ref[1] = im
    if tiled:
        tile_ref = refs[1]
        slabs, _, rows, cols = tile_ref.shape
        for g in range(slabs // across):
            for c in range(across):
                for j, x in enumerate((re, im)):
                    tile_ref[g * across + c, j] = x[
                        g * rows : (g + 1) * rows, c * cols : (c + 1) * cols
                    ]


def product(terms, panel, base, at, n, into=None, finish=False, tiled=False):
    like = terms[0][0][0]
    cols = base.shape[2]
    across = cols // like.shape[3]
    per = cols // panel.shape[2]
    full = lambda shape: pl.BlockSpec(shape, lambda i, b: (0,) * len(shape))
    band = lambda rows: pl.BlockSpec((2, n, cols), lambda i, b: (0, 0 if rows == n else at // n, 0))
    out_rows = panel.shape[2] if finish else n
    outs = [jax.ShapeDtypeStruct((2, out_rows, cols), jnp.float32)]
    out_specs = [band(out_rows)]
    if tiled:
        outs.append(jax.ShapeDtypeStruct(like.shape, jnp.float32))
        out_specs.append(full(like.shape))
    in_specs, ins = [], []
    for j, (lefts, _) in enumerate(terms):
        in_specs += [full(x.shape) for x in lefts]
        in_specs.append(
            pl.BlockSpec((per,) + panel.shape[1:], lambda i, b, j=j: (b[j], 0, 0, 0))
        )
        ins += list(lefts) + [panel]
    in_specs.append(band(base.shape[1]))
    ins.append(base)
    counts = [len(x) for x, _ in terms]
    aliases = {}
    skip = into is not None
    if skip:
        aliases = {len(ins) + 1: 0}
        in_specs.append(pl.BlockSpec(memory_space=pl.ANY))
        ins.append(into)
    res = pl.pallas_call(
        lambda *refs: product_kernel(counts, across, tiled, skip, *refs),
        out_shape=outs,
        grid_spec=pltpu.PrefetchScalarGridSpec(
            num_scalar_prefetch=1, grid=(1,), in_specs=in_specs, out_specs=out_specs
        ),
        input_output_aliases=aliases,
        compiler_params=pltpu.CompilerParams(vmem_limit_bytes=VMEM),
        name="product_tiled" if tiled else "product",
    )(jnp.stack([block for _, block in terms]), *ins)
    return res if tiled else res[0]


def time_product(sigma, panel, base, at, n, into, tiled):
    zl = lax.axis_index("zl")
    low = zl < 2
    near = lax.ppermute(sigma, "zl", [(0, 1), (1, 0), (2, 3), (3, 2)])
    mid = lax.ppermute(sigma, "zl", [(1, 2), (2, 1)])
    end_two = lax.ppermute(mid, "zl", [(1, 0), (2, 3)])
    mid_far = lax.ppermute(near, "zl", [(1, 2), (2, 1)])
    end_far = lax.ppermute(mid_far, "zl", [(1, 0), (2, 3)])
    total = product([([sigma], zl), ([near], lax.bitwise_xor(zl, 1))], panel, base, at, n)
    terms = [([mid, end_two], jnp.where(low, 2, 1)), ([mid_far, end_far], jnp.where(low, 3, 0))]
    return product(terms, panel, total, at, n, into, True, tiled)


def exchange(x):
    return lax.all_to_all(x, ("zh", "y"), 0, 0, tiled=True)


def slabs_kernel(at, across, free_ref, greater_ref, out_ref):
    slabs, _, rows, cols = out_ref.shape
    for j, ref in enumerate((free_ref, free_ref, greater_ref, greater_ref)):
        for g in range(slabs // across):
            band = ref[j % 2, pl.ds(at + g * rows, rows)]
            for c in range(across):
                out_ref[g * across + c, j] = band[:, c * cols : (c + 1) * cols]


def to_slabs(free, greater, at, n, momenta):
    across = free.shape[2] // LANES
    out = jax.ShapeDtypeStruct((momenta, 4, n * across // momenta, LANES), jnp.float32)
    vmem = pl.BlockSpec(memory_space=pltpu.VMEM)
    return pl.pallas_call(
        lambda *refs: slabs_kernel(at, across, *refs),
        out_shape=out,
        in_specs=[vmem, vmem],
        out_specs=vmem,
        compiler_params=pltpu.CompilerParams(vmem_limit_bytes=VMEM),
        name="to_slabs",
    )(free, greater)


def body(g_free, g_greater_t, momentum_map, weights):
    momenta = momentum_map.shape[0]
    free, greater = g_free[:, 0], g_greater_t[:, 0]
    weights = weights.reshape(-1, 1, LANES)
    panel = lax.all_gather(free, ("x", "core"))
    starts = [sum(CHUNKS[:i]) for i in range(len(CHUNKS))]

    sigmas, mirrors = [], []
    fields = [exchange(to_slabs(free, greater, at, n, momenta)) for at, n in zip(starts, CHUNKS)]
    for field in fields:
        sigma, mirror = self_energy(momentum_map, weights, field)
        sigmas.append(exchange(sigma))
        mirrors.append(mirror)
    for sweep in range(ITERS):
        last = sweep == ITERS - 1
        green, fields = None, []
        for sigma, at, n in zip(sigmas, starts, CHUNKS):
            green = time_product(sigma, panel, free, at, n, green, not last)
            if not last:
                green, tiles = green
                fields.append(exchange(tiles))
        if last:
            return green[:, None]
        panel = lax.all_gather(green, ("x", "core"))
        sigmas = [
            exchange(self_energy(momentum_map, weights, f, m)) for f, m in zip(fields, mirrors)
        ]


def solution(mesh):
    fine = Mesh(mesh.devices.reshape(3, 8, 4, 4, 2), ("zh", "y", "zl", "x", "core"))
    spec = P(None, ("zh", "y"), ("x", "core"), "zl")
    return jax.shard_map(
        body, mesh=fine, in_specs=(spec, spec, P(), P()), out_specs=spec, check_vma=False
    )
```

```python
import math

import jax
import jax.numpy as jnp
from jax import lax
from jax.experimental import pallas as pl
from jax.experimental.pallas import tpu as pltpu
from jax.sharding import Mesh, PartitionSpec as P

LY = 4
ITERS = 2


CHUNKS = 2
VMEM = 24 * 1024 * 1024

LANES = 128
ROOT3_2 = math.sqrt(3.0) / 2.0


def c_add(a, b):
    return (a[0] + b[0], a[1] + b[1])


def c_sub(a, b):
    return (a[0] - b[0], a[1] - b[1])


def c_turn(a, sign):
    return (-a[1], a[0]) if sign > 0 else (a[1], -a[0])


def dft3(x0, x1, x2, sign):
    u = c_add(x1, x2)
    v = c_sub(x1, x2)
    m = (x0[0] - 0.5 * u[0], x0[1] - 0.5 * u[1])
    n = c_turn((ROOT3_2 * v[0], ROOT3_2 * v[1]), sign)
    return c_add(x0, u), c_add(m, n), c_sub(m, n)


def dft4(x, sign):
    t0, t1 = c_add(x[0], x[2]), c_sub(x[0], x[2])
    t2, t3 = c_add(x[1], x[3]), c_turn(c_sub(x[1], x[3]), sign)
    return [c_add(t0, t2), c_add(t1, t3), c_sub(t0, t2), c_sub(t1, t3)]


def dft6(x, sign):
    b = [c_add(x[m], x[m + 3]) for m in range(3)]
    c = [c_sub(x[m], x[m + 3]) for m in range(3)]
    even = dft3(b[0], b[1], b[2], sign)
    odd = dft3(c[0], (-c[1][0], -c[1][1]), c[2], sign)
    return [even[0], odd[2], even[1], odd[0], even[2], odd[1]]


def lattice_transform(x, sign):
    rows = [[None] * 6 for _ in range(4)]
    for across in range(6):
        column = dft4([x[6 * down + across] for down in range(4)], sign)
        for down in range(4):
            rows[down][across] = column[down]
    out = []
    for down in range(4):
        out.extend(dft6(rows[down], sign))
    return out


def self_energy_kernel(first, map_ref, weights_ref, field_ref, *refs):
    if first:
        sigma_ref, mirror_ref, where_ref = refs
    else:
        mirror_ref, sigma_ref, where_ref = refs
    momenta = field_ref.shape[0]
    for k in range(momenta):
        where_ref[map_ref[k]] = k
    spot = [where_ref[q] for q in range(momenta)]
    zl = lax.axis_index("zl")
    for lane in range(0, field_ref.shape[3], LANES):
        cut = pl.ds(lane, LANES)
        if first:
            mirror = lattice_transform(
                [(field_ref[k, 2, :, cut], field_ref[k, 3, :, cut]) for k in spot], -1
            )
            scale = 1.0 / (momenta * momenta)
            for r in range(momenta):
                mirror_ref[r, 0, :, cut] = mirror[r][0] * scale
                mirror_ref[r, 1, :, cut] = mirror[r][1] * scale
        space = lattice_transform(
            [(field_ref[k, 0, :, cut], field_ref[k, 1, :, cut]) for k in spot], 1
        )
        source = []
        for r in range(momenta):
            re, im = space[r]
            sq_re = re * re - im * im
            sq_im = 2.0 * re * im
            m_re, m_im = mirror_ref[r, 0, :, cut], mirror_ref[r, 1, :, cut]
            source.append((sq_re * m_re - sq_im * m_im, sq_re * m_im + sq_im * m_re))
        sigma = lattice_transform(source, -1)
        w = weights_ref[zl, :, cut]
        for q in range(momenta):
            sigma_ref[spot[q], 0, :, cut] = sigma[q][0] * w
            sigma_ref[spot[q], 1, :, cut] = sigma[q][1] * w


def self_energy(momentum_map, weights, field, mirror=None):
    first = mirror is None
    momenta, _, rows, cols = field.shape
    shape = jax.ShapeDtypeStruct((momenta, 2, rows, cols), jnp.float32)
    smem = pl.BlockSpec(memory_space=pltpu.SMEM)
    vmem = pl.BlockSpec(memory_space=pltpu.VMEM)
    ins = [momentum_map, weights, field] + ([] if first else [mirror])
    return pl.pallas_call(
        lambda *refs: self_energy_kernel(first, *refs),
        out_shape=(shape, shape) if first else shape,
        in_specs=[smem] + [vmem] * (len(ins) - 1),
        out_specs=(vmem, vmem) if first else vmem,
        scratch_shapes=[pltpu.SMEM((momenta,), jnp.int32)],
        compiler_params=pltpu.CompilerParams(vmem_limit_bytes=VMEM),
        name="self_energy_first" if first else "self_energy_next",
    )(*ins)


def split_left(x):
    hi = x.astype(jnp.bfloat16)
    lo = (x - hi.astype(jnp.float32)).astype(jnp.bfloat16)
    return jnp.concatenate([hi, lo, hi], axis=1)


def split_right(x):
    hi = x.astype(jnp.bfloat16)
    lo = (x - hi.astype(jnp.float32)).astype(jnp.bfloat16)
    return jnp.concatenate([hi, hi, lo], axis=0)


def mul(a, b):
    return jnp.dot(split_left(a), split_right(b), preferred_element_type=jnp.float32)


def product_kernel(n_lefts, blocks_ref, *refs):
    lefts, panels, refs = refs[:n_lefts], refs[n_lefts : 2 * n_lefts], refs[2 * n_lefts :]
    out_ref = refs[-1]

    def flat(x):
        return x.reshape(x.shape[0] * x.shape[1], x.shape[2])

    re = im = None
    if len(refs) == 2:
        re, im = refs[0][0], refs[0][1]
    for left_ref, panel_ref in zip(lefts, panels):
        s_re, s_im = flat(left_ref[:, 0]), flat(left_ref[:, 1])
        g_re, g_im = flat(panel_ref[:, 0]), flat(panel_ref[:, 1])
        one = mul(s_re, g_re)
        two = mul(s_im, g_im)
        three = mul(s_re + s_im, g_re + g_im)
        if re is None:
            re, im = one - two, three - one - two
        else:
            re, im = re + (one - two), im + (three - one - two)
    out_ref[0] = re
    out_ref[1] = im


def product(lefts, panel, blocks, base=None, chunk=0):
    slabs, _, high, cols = lefts[0].shape
    rows = slabs * high
    per = cols // panel.shape[2]
    full = lambda shape: pl.BlockSpec(shape, lambda i, b: (0,) * len(shape))
    in_specs = [full(x.shape) for x in lefts]
    for j in range(len(lefts)):
        in_specs.append(
            pl.BlockSpec((per,) + panel.shape[1:], lambda i, b, j=j: (b[j], 0, 0, 0))
        )
    ins = list(lefts) + [panel] * len(lefts)
    if base is not None:
        in_specs.append(pl.BlockSpec((2, rows, cols), lambda i, b: (0, chunk, 0)))
        ins.append(base)
    return pl.pallas_call(
        lambda *refs: product_kernel(len(lefts), *refs),
        out_shape=jax.ShapeDtypeStruct((2, rows, cols), jnp.float32),
        grid_spec=pltpu.PrefetchScalarGridSpec(
            num_scalar_prefetch=1,
            grid=(1,),
            in_specs=in_specs,
            out_specs=full((2, rows, cols)),
        ),
        compiler_params=pltpu.CompilerParams(vmem_limit_bytes=VMEM),
        name="product_other" if base is None else "product_own",
    )(blocks, *ins)


def finish_kernel(n, tiled, *refs):
    own, other, outs = refs[:n], refs[n : 2 * n], refs[2 * n :]
    rows = own[0].shape[1]
    for i in range(n):
        for j in range(2):
            x = own[i][j] + other[i][j]
            outs[0][j, i * rows : (i + 1) * rows] = x
            if tiled:
                slabs, _, high, cols = outs[1].shape
                outs[1][i * slabs // n : (i + 1) * slabs // n, j] = x.reshape(
                    slabs // n, high, cols
                )


def finish(own, other, tiles):
    n = len(own)
    _, rows, cols = own[0].shape
    outs = [jax.ShapeDtypeStruct((2, n * rows, cols), jnp.float32)]
    if tiles is not None:
        outs.append(jax.ShapeDtypeStruct(tiles, jnp.float32))
    vmem = pl.BlockSpec(memory_space=pltpu.VMEM)
    return pl.pallas_call(
        lambda *refs: finish_kernel(n, tiles is not None, *refs),
        out_shape=outs,
        in_specs=[vmem] * (2 * n),
        out_specs=[vmem] * len(outs),
        compiler_params=pltpu.CompilerParams(vmem_limit_bytes=VMEM),
        name="finish_tiled" if tiles is not None else "finish",
    )(*own, *other)


def time_product(sigma, panel, free, tiled):
    zl = lax.axis_index("zl")
    turn = lambda by: lax.bitwise_xor(zl, by)
    own_blocks = jnp.stack([zl, turn(2)])
    other_blocks = jnp.stack([turn(1), turn(3)])
    slabs = sigma.shape[0] // CHUNKS
    mine = [sigma[i * slabs : (i + 1) * slabs] for i in range(CHUNKS)]
    swapped = [lax.ppermute(x, "zl", [(0, 2), (1, 3), (2, 0), (3, 1)]) for x in mine]
    own, other = [], []
    for i, pair in enumerate(zip(mine, swapped)):
        part = product(pair, panel, other_blocks)
        other.append(lax.ppermute(part, "zl", [(0, 1), (1, 0), (2, 3), (3, 2)]))
        own.append(product(pair, panel, own_blocks, free, i))
    return finish(own, other, sigma.shape if tiled else None)


def pack_kernel(free_ref, greater_ref, out_ref, sems):
    copies = []
    for j, ref in enumerate((free_ref, free_ref, greater_ref, greater_ref)):
        copies.append(pltpu.make_async_copy(ref.at[j % 2], out_ref.at[:, j], sems.at[j]))
    for copy in copies:
        copy.start()
    for copy in copies:
        copy.wait()


def pack(free, greater):
    _, slabs, high, cols = free.shape
    hbm = pl.BlockSpec(memory_space=pltpu.HBM)
    return pl.pallas_call(
        pack_kernel,
        out_shape=jax.ShapeDtypeStruct((slabs, 4, high, cols), jnp.float32),
        in_specs=[hbm, hbm],
        out_specs=hbm,
        scratch_shapes=[pltpu.SemaphoreType.DMA((4,))],
        compiler_params=pltpu.CompilerParams(vmem_limit_bytes=VMEM),
        name="pack",
    )(*(pltpu.with_memory_space_constraint(x, pltpu.HBM) for x in (free, greater)))


def exchange(x):
    return lax.all_to_all(x, ("zh", "y"), 0, 0, tiled=True)


def spread(tile):
    nx = lax.axis_size("x")
    moves = []
    for zl in range(lax.axis_size("zl")):
        for x in range(nx):
            stays = x % 2 == zl % 2
            to = (zl, x) if stays else (zl ^ 1, x ^ 1)
            moves.append((zl * nx + x, to[0] * nx + to[1]))
    return lax.ppermute(tile, ("zl", "x"), moves)


def body(g_free, g_greater_t, momentum_map, weights):
    momenta = momentum_map.shape[0]
    free, greater = g_free[:, 0], g_greater_t[:, 0]
    tile_rows, tile_cols = free.shape[1:]
    slabs = (2, momenta, tile_rows // momenta, tile_cols)
    weights = weights.reshape(-1, 1, tile_cols)

    moved = spread(free)
    field = exchange(pack(free.reshape(slabs), greater.reshape(slabs)))
    mirror = None
    for sweep in range(ITERS):
        field, moved = lax.optimization_barrier((field, moved))
        panel = pltpu.with_memory_space_constraint(
            lax.all_gather(moved, ("x", "core")), pltpu.HBM
        )
        if mirror is None:
            sigma, mirror = self_energy(momentum_map, weights, field)
        else:
            sigma = self_energy(momentum_map, weights, field, mirror)
        sigma = exchange(sigma)
        if sweep == ITERS - 1:
            return time_product(sigma, panel, free, False)[0][:, None]
        green, tiles = time_product(sigma, panel, free, True)
        moved = spread(green)
        field = exchange(tiles)


def solution(mesh):
    fine = Mesh(mesh.devices.reshape(3, 8, 4, 4, 2), ("zh", "y", "zl", "x", "core"))
    spec = P(None, ("zh", "y"), ("x", "core"), "zl")
    return jax.shard_map(
        body, mesh=fine, in_specs=(spec, spec, P(), P()), out_specs=spec, check_vma=False
    )
```

```python
import math

import jax
import jax.numpy as jnp
from jax import lax
from jax.experimental import pallas as pl
from jax.experimental.pallas import tpu as pltpu
from jax.sharding import Mesh, PartitionSpec as P


ITERS = 2


CHUNKS = 2
VMEM = 24 * 1024 * 1024

LANES = 128
ROOT3_2 = math.sqrt(3.0) / 2.0


def c_add(a, b):
    return (a[0] + b[0], a[1] + b[1])


def c_sub(a, b):
    return (a[0] - b[0], a[1] - b[1])


def c_turn(a, sign):
    return (-a[1], a[0]) if sign > 0 else (a[1], -a[0])


def dft3(x0, x1, x2, sign):
    u = c_add(x1, x2)
    v = c_sub(x1, x2)
    m = (x0[0] - 0.5 * u[0], x0[1] - 0.5 * u[1])
    n = c_turn((ROOT3_2 * v[0], ROOT3_2 * v[1]), sign)
    return c_add(x0, u), c_add(m, n), c_sub(m, n)


def dft4(x, sign):
    t0, t1 = c_add(x[0], x[2]), c_sub(x[0], x[2])
    t2, t3 = c_add(x[1], x[3]), c_turn(c_sub(x[1], x[3]), sign)
    return [c_add(t0, t2), c_add(t1, t3), c_sub(t0, t2), c_sub(t1, t3)]


def dft6(x, sign):
    b = [c_add(x[m], x[m + 3]) for m in range(3)]
    c = [c_sub(x[m], x[m + 3]) for m in range(3)]
    even = dft3(b[0], b[1], b[2], sign)
    odd = dft3(c[0], (-c[1][0], -c[1][1]), c[2], sign)
    return [even[0], odd[2], even[1], odd[0], even[2], odd[1]]


def lattice_transform(x, sign):
    rows = [[None] * 6 for _ in range(4)]
    for across in range(6):
        column = dft4([x[6 * down + across] for down in range(4)], sign)
        for down in range(4):
            rows[down][across] = column[down]
    out = []
    for down in range(4):
        out.extend(dft6(rows[down], sign))
    return out


def self_energy_kernel(first, map_ref, weights_ref, field_ref, *refs):
    if first:
        sigma_ref, mirror_ref, where_ref = refs
    else:
        mirror_ref, sigma_ref, where_ref = refs
    momenta = field_ref.shape[0]
    for k in range(momenta):
        where_ref[map_ref[k]] = k
    spot = [where_ref[q] for q in range(momenta)]
    zl = lax.axis_index("zl")
    for lane in range(0, field_ref.shape[3], LANES):
        cut = pl.ds(lane, LANES)
        if first:
            mirror = lattice_transform(
                [(field_ref[k, 2, :, cut], field_ref[k, 3, :, cut]) for k in spot], -1
            )
            scale = 1.0 / (momenta * momenta)
            for r in range(momenta):
                mirror_ref[r, 0, :, cut] = mirror[r][0] * scale
                mirror_ref[r, 1, :, cut] = mirror[r][1] * scale
        space = lattice_transform(
            [(field_ref[k, 0, :, cut], field_ref[k, 1, :, cut]) for k in spot], 1
        )
        source = []
        for r in range(momenta):
            re, im = space[r]
            sq_re = re * re - im * im
            sq_im = 2.0 * re * im
            m_re, m_im = mirror_ref[r, 0, :, cut], mirror_ref[r, 1, :, cut]
            source.append((sq_re * m_re - sq_im * m_im, sq_re * m_im + sq_im * m_re))
        sigma = lattice_transform(source, -1)
        w = weights_ref[zl, :, cut]
        for q in range(momenta):
            sigma_ref[spot[q], 0, :, cut] = sigma[q][0] * w
            sigma_ref[spot[q], 1, :, cut] = sigma[q][1] * w


def self_energy(momentum_map, weights, field, mirror=None):
    first = mirror is None
    momenta, _, rows, cols = field.shape
    shape = jax.ShapeDtypeStruct((momenta, 2, rows, cols), jnp.float32)
    smem = pl.BlockSpec(memory_space=pltpu.SMEM)
    vmem = pl.BlockSpec(memory_space=pltpu.VMEM)
    ins = [momentum_map, weights, field] + ([] if first else [mirror])
    return pl.pallas_call(
        lambda *refs: self_energy_kernel(first, *refs),
        out_shape=(shape, shape) if first else shape,
        in_specs=[smem] + [vmem] * (len(ins) - 1),
        out_specs=(vmem, vmem) if first else vmem,
        scratch_shapes=[pltpu.SMEM((momenta,), jnp.int32)],
        compiler_params=pltpu.CompilerParams(vmem_limit_bytes=VMEM),
        name="self_energy_first" if first else "self_energy_next",
    )(*ins)


def split_left(x):
    hi = x.astype(jnp.bfloat16)
    lo = (x - hi.astype(jnp.float32)).astype(jnp.bfloat16)
    return jnp.concatenate([hi, lo, hi], axis=1)


def split_right(x):
    hi = x.astype(jnp.bfloat16)
    lo = (x - hi.astype(jnp.float32)).astype(jnp.bfloat16)
    return jnp.concatenate([hi, hi, lo], axis=0)


def mul(a, b):
    return jnp.dot(split_left(a), split_right(b), preferred_element_type=jnp.float32)


def product_kernel(n_lefts, blocks_ref, *refs):
    lefts, panels, refs = refs[:n_lefts], refs[n_lefts : 2 * n_lefts], refs[2 * n_lefts :]
    out_ref = refs[-1]

    def flat(x):
        return x.reshape(x.shape[0] * x.shape[1], x.shape[2])

    re = im = None
    if len(refs) == 2:
        re, im = refs[0][0], refs[0][1]
    for left_ref, panel_ref in zip(lefts, panels):
        s_re, s_im = flat(left_ref[:, 0]), flat(left_ref[:, 1])
        g_re, g_im = flat(panel_ref[:, 0]), flat(panel_ref[:, 1])
        one = mul(s_re, g_re)
        two = mul(s_im, g_im)
        three = mul(s_re + s_im, g_re + g_im)
        if re is None:
            re, im = one - two, three - one - two
        else:
            re, im = re + (one - two), im + (three - one - two)
    out_ref[0] = re
    out_ref[1] = im


def product(lefts, panel, blocks, base=None, chunk=0):
    slabs, _, high, cols = lefts[0].shape
    rows = slabs * high
    per = cols // panel.shape[2]
    full = lambda shape: pl.BlockSpec(shape, lambda i, b: (0,) * len(shape))
    in_specs = [full(x.shape) for x in lefts]
    for j in range(len(lefts)):
        in_specs.append(
            pl.BlockSpec((per,) + panel.shape[1:], lambda i, b, j=j: (b[j], 0, 0, 0))
        )
    ins = list(lefts) + [panel] * len(lefts)
    if base is not None:
        in_specs.append(pl.BlockSpec((2, rows, cols), lambda i, b: (0, chunk, 0)))
        ins.append(base)
    return pl.pallas_call(
        lambda *refs: product_kernel(len(lefts), *refs),
        out_shape=jax.ShapeDtypeStruct((2, rows, cols), jnp.float32),
        grid_spec=pltpu.PrefetchScalarGridSpec(
            num_scalar_prefetch=1,
            grid=(1,),
            in_specs=in_specs,
            out_specs=full((2, rows, cols)),
        ),
        compiler_params=pltpu.CompilerParams(vmem_limit_bytes=VMEM),
        name="product_other" if base is None else "product_own",
    )(blocks, *ins)


def finish_kernel(n, tiled, *refs):
    own, other, outs = refs[:n], refs[n : 2 * n], refs[2 * n :]
    rows = own[0].shape[1]
    for i in range(n):
        for j in range(2):
            x = own[i][j] + other[i][j]
            outs[0][j, i * rows : (i + 1) * rows] = x
            if tiled:
                slabs, _, high, cols = outs[1].shape
                outs[1][i * slabs // n : (i + 1) * slabs // n, j] = x.reshape(
                    slabs // n, high, cols
                )


def finish(own, other, tiles):
    n = len(own)
    _, rows, cols = own[0].shape
    outs = [jax.ShapeDtypeStruct((2, n * rows, cols), jnp.float32)]
    if tiles is not None:
        outs.append(jax.ShapeDtypeStruct(tiles, jnp.float32))
    vmem = pl.BlockSpec(memory_space=pltpu.VMEM)
    return pl.pallas_call(
        lambda *refs: finish_kernel(n, tiles is not None, *refs),
        out_shape=outs,
        in_specs=[vmem] * (2 * n),
        out_specs=[vmem] * len(outs),
        compiler_params=pltpu.CompilerParams(vmem_limit_bytes=VMEM),
        name="finish_tiled" if tiles is not None else "finish",
    )(*own, *other)


def time_product(sigma, panel, free, tiled):
    zl = lax.axis_index("zl")
    turn = lambda by: lax.bitwise_xor(zl, by)
    own_blocks = jnp.stack([zl, turn(2)])
    other_blocks = jnp.stack([turn(1), turn(3)])
    slabs = sigma.shape[0] // CHUNKS
    mine = [sigma[i * slabs : (i + 1) * slabs] for i in range(CHUNKS)]
    swapped = [lax.ppermute(x, "zl", [(0, 2), (1, 3), (2, 0), (3, 1)]) for x in mine]
    own, other = [], []
    for i, (left, right) in enumerate(zip(mine, swapped)):
        if own:
            right, own[-1], _ = lax.optimization_barrier((right, own[-1], part))
        pair = (left, right)
        part = product(pair, panel, other_blocks)
        other.append(lax.ppermute(part, "zl", [(0, 1), (1, 0), (2, 3), (3, 2)]))
        own.append(product(pair, panel, own_blocks, free, i))
    return finish(own, other, sigma.shape if tiled else None)


def pack_kernel(free_ref, greater_ref, out_ref):
    for j in range(2):
        out_ref[:, j] = free_ref[j]
        out_ref[:, 2 + j] = greater_ref[j]


def pack(free, greater):
    _, slabs, high, cols = free.shape
    step = slabs // 4
    block = pl.BlockSpec((2, step, high, cols), lambda i: (0, i, 0, 0))
    return pl.pallas_call(
        pack_kernel,
        out_shape=jax.ShapeDtypeStruct((slabs, 4, high, cols), jnp.float32),
        grid=(4,),
        in_specs=[block, block],
        out_specs=pl.BlockSpec((step, 4, high, cols), lambda i: (i, 0, 0, 0)),
        compiler_params=pltpu.CompilerParams(vmem_limit_bytes=VMEM),
        name="pack",
    )(*(pltpu.with_memory_space_constraint(x, pltpu.HBM) for x in (free, greater)))


def exchange(x):
    return lax.all_to_all(x, ("zh", "y"), 0, 0, tiled=True)


def spread(tile):
    nx = lax.axis_size("x")
    moves = []
    for zl in range(lax.axis_size("zl")):
        for x in range(nx):
            stays = x % 2 == zl % 2
            to = (zl, x) if stays else (zl ^ 1, x ^ 1)
            moves.append((zl * nx + x, to[0] * nx + to[1]))
    return lax.ppermute(tile, ("zl", "x"), moves)


def body(g_free, g_greater_t, momentum_map, weights):
    momenta = momentum_map.shape[0]
    free, greater = g_free[:, 0], g_greater_t[:, 0]
    tile_rows, tile_cols = free.shape[1:]
    slabs = (2, momenta, tile_rows // momenta, tile_cols)
    weights = weights.reshape(-1, 1, tile_cols)

    moved = spread(free)
    both = pack(free.reshape(slabs), greater.reshape(slabs))
    field = exchange(both)
    mirror = None
    for sweep in range(ITERS):
        moved = settle(moved)
        panel = lax.all_gather(moved, ("x", "core"))
        panel = pltpu.with_memory_space_constraint(panel, pltpu.HBM)
        if mirror is None:
            sigma, mirror = self_energy(momentum_map, weights, field)
        else:
            sigma = self_energy(momentum_map, weights, field, mirror)
        sigma = exchange(sigma)
        if sweep == ITERS - 1:
            return time_product(sigma, panel, free, False)[0][:, None]
        green, tiles = time_product(sigma, panel, free, True)
        moved = spread(green)
        field = exchange(tiles)


def settle(tile):
    def kernel(tile_ref, out_ref):
        out_ref[...] = tile_ref[...]

    return pl.pallas_call(
        kernel,
        out_shape=jax.ShapeDtypeStruct(tile.shape, tile.dtype),
        compiler_params=pltpu.CompilerParams(vmem_limit_bytes=VMEM),
        name="settle",
    )(tile)


def solution(mesh):
    fine = Mesh(mesh.devices.reshape(3, 8, 4, 4, 2), ("zh", "y", "zl", "x", "core"))
    spec = P(None, ("zh", "y"), ("x", "core"), "zl")
    return jax.shard_map(
        body, mesh=fine, in_specs=(spec, spec, P(), P()), out_specs=spec, check_vma=False
    )
```

```python
import math

import jax
import jax.numpy as jnp
from jax import lax
from jax.experimental import pallas as pl
from jax.experimental.pallas import tpu as pltpu
from jax.sharding import Mesh, PartitionSpec as P


ITERS = 2


CHUNKS = 2
ZL = ("h", "l")
VMEM = 24 * 1024 * 1024

LANES = 128
ROOT3_2 = math.sqrt(3.0) / 2.0


def c_add(a, b):
    return (a[0] + b[0], a[1] + b[1])


def c_sub(a, b):
    return (a[0] - b[0], a[1] - b[1])


def c_turn(a, sign):
    return (-a[1], a[0]) if sign > 0 else (a[1], -a[0])


def dft3(x0, x1, x2, sign):
    u = c_add(x1, x2)
    v = c_sub(x1, x2)
    m = (x0[0] - 0.5 * u[0], x0[1] - 0.5 * u[1])
    n = c_turn((ROOT3_2 * v[0], ROOT3_2 * v[1]), sign)
    return c_add(x0, u), c_add(m, n), c_sub(m, n)


def dft4(x, sign):
    t0, t1 = c_add(x[0], x[2]), c_sub(x[0], x[2])
    t2, t3 = c_add(x[1], x[3]), c_turn(c_sub(x[1], x[3]), sign)
    return [c_add(t0, t2), c_add(t1, t3), c_sub(t0, t2), c_sub(t1, t3)]


def dft6(x, sign):
    b = [c_add(x[m], x[m + 3]) for m in range(3)]
    c = [c_sub(x[m], x[m + 3]) for m in range(3)]
    even = dft3(b[0], b[1], b[2], sign)
    odd = dft3(c[0], (-c[1][0], -c[1][1]), c[2], sign)
    return [even[0], odd[2], even[1], odd[0], even[2], odd[1]]


def lattice_transform(x, sign):
    rows = [[None] * 6 for _ in range(4)]
    for across in range(6):
        column = dft4([x[6 * down + across] for down in range(4)], sign)
        for down in range(4):
            rows[down][across] = column[down]
    out = []
    for down in range(4):
        out.extend(dft6(rows[down], sign))
    return out


def self_energy_kernel(first, map_ref, weights_ref, field_ref, *refs):
    if first:
        sigma_ref, mirror_ref, where_ref = refs
    else:
        mirror_ref, sigma_ref, where_ref = refs
    momenta = field_ref.shape[0]
    for k in range(momenta):
        where_ref[map_ref[k]] = k
    spot = [where_ref[q] for q in range(momenta)]
    zl = lax.axis_index(ZL)
    for lane in range(0, field_ref.shape[3], LANES):
        cut = pl.ds(lane, LANES)
        if first:
            mirror = lattice_transform(
                [(field_ref[k, 2, :, cut], field_ref[k, 3, :, cut]) for k in spot], -1
            )
            scale = 1.0 / (momenta * momenta)
            for r in range(momenta):
                mirror_ref[r, 0, :, cut] = mirror[r][0] * scale
                mirror_ref[r, 1, :, cut] = mirror[r][1] * scale
        space = lattice_transform(
            [(field_ref[k, 0, :, cut], field_ref[k, 1, :, cut]) for k in spot], 1
        )
        source = []
        for r in range(momenta):
            re, im = space[r]
            sq_re = re * re - im * im
            sq_im = 2.0 * re * im
            m_re, m_im = mirror_ref[r, 0, :, cut], mirror_ref[r, 1, :, cut]
            source.append((sq_re * m_re - sq_im * m_im, sq_re * m_im + sq_im * m_re))
        sigma = lattice_transform(source, -1)
        w = weights_ref[zl, :, cut]
        for q in range(momenta):
            sigma_ref[spot[q], 0, :, cut] = sigma[q][0] * w
            sigma_ref[spot[q], 1, :, cut] = sigma[q][1] * w


def self_energy(momentum_map, weights, field, mirror=None):
    first = mirror is None
    momenta, _, rows, cols = field.shape
    shape = jax.ShapeDtypeStruct((momenta, 2, rows, cols), jnp.float32)
    smem = pl.BlockSpec(memory_space=pltpu.SMEM)
    vmem = pl.BlockSpec(memory_space=pltpu.VMEM)
    ins = [momentum_map, weights, field] + ([] if first else [mirror])
    return pl.pallas_call(
        lambda *refs: self_energy_kernel(first, *refs),
        out_shape=(shape, shape) if first else shape,
        in_specs=[smem] + [vmem] * (len(ins) - 1),
        out_specs=(vmem, vmem) if first else vmem,
        scratch_shapes=[pltpu.SMEM((momenta,), jnp.int32)],
        compiler_params=pltpu.CompilerParams(vmem_limit_bytes=VMEM),
        name="self_energy_first" if first else "self_energy_next",
    )(*ins)


def split_left(x):
    hi = x.astype(jnp.bfloat16)
    lo = (x - hi.astype(jnp.float32)).astype(jnp.bfloat16)
    return jnp.concatenate([hi, lo, hi], axis=1)


def split_right(x):
    hi = x.astype(jnp.bfloat16)
    lo = (x - hi.astype(jnp.float32)).astype(jnp.bfloat16)
    return jnp.concatenate([hi, hi, lo], axis=0)


def mul(a, b):
    return jnp.dot(split_left(a), split_right(b), preferred_element_type=jnp.float32)


def product_kernel(n_lefts, blocks_ref, *refs):
    lefts, panels, refs = refs[:n_lefts], refs[n_lefts : 2 * n_lefts], refs[2 * n_lefts :]
    out_ref = refs[-1]

    def flat(x):
        return x.reshape(x.shape[0] * x.shape[1], x.shape[2])

    re = im = None
    if len(refs) == 2:
        re, im = refs[0][0], refs[0][1]
    for left_ref, panel_ref in zip(lefts, panels):
        s_re, s_im = flat(left_ref[:, 0]), flat(left_ref[:, 1])
        g_re, g_im = flat(panel_ref[:, 0]), flat(panel_ref[:, 1])
        one = mul(s_re, g_re)
        two = mul(s_im, g_im)
        three = mul(s_re + s_im, g_re + g_im)
        if re is None:
            re, im = one - two, three - one - two
        else:
            re, im = re + (one - two), im + (three - one - two)
    out_ref[0] = re
    out_ref[1] = im


def product(lefts, panel, blocks, base=None, chunk=0):
    slabs, _, high, cols = lefts[0].shape
    rows = slabs * high
    per = cols // panel.shape[2]
    full = lambda shape: pl.BlockSpec(shape, lambda i, b: (0,) * len(shape))
    in_specs = [full(x.shape) for x in lefts]
    for j in range(len(lefts)):
        in_specs.append(
            pl.BlockSpec((per,) + panel.shape[1:], lambda i, b, j=j: (b[j], 0, 0, 0))
        )
    ins = list(lefts) + [panel] * len(lefts)
    if base is not None:
        in_specs.append(pl.BlockSpec((2, rows, cols), lambda i, b: (0, chunk, 0)))
        ins.append(base)
    return pl.pallas_call(
        lambda *refs: product_kernel(len(lefts), *refs),
        out_shape=jax.ShapeDtypeStruct((2, rows, cols), jnp.float32),
        grid_spec=pltpu.PrefetchScalarGridSpec(
            num_scalar_prefetch=1,
            grid=(1,),
            in_specs=in_specs,
            out_specs=full((2, rows, cols)),
        ),
        compiler_params=pltpu.CompilerParams(vmem_limit_bytes=VMEM),
        name="product_other" if base is None else "product_own",
    )(blocks, *ins)


def finish_kernel(n, tiled, *refs):
    own, other, outs = refs[:n], refs[n : 2 * n], refs[2 * n :]
    rows = own[0].shape[1]
    for i in range(n):
        for j in range(2):
            x = own[i][j] + other[i][j]
            outs[0][j, i * rows : (i + 1) * rows] = x
            if tiled:
                slabs, _, high, cols = outs[1].shape
                outs[1][i * slabs // n : (i + 1) * slabs // n, j] = x.reshape(
                    slabs // n, high, cols
                )


def finish(own, other, tiles):
    n = len(own)
    _, rows, cols = own[0].shape
    outs = [jax.ShapeDtypeStruct((2, n * rows, cols), jnp.float32)]
    if tiles is not None:
        outs.append(jax.ShapeDtypeStruct(tiles, jnp.float32))
    vmem = pl.BlockSpec(memory_space=pltpu.VMEM)
    return pl.pallas_call(
        lambda *refs: finish_kernel(n, tiles is not None, *refs),
        out_shape=outs,
        in_specs=[vmem] * (2 * n),
        out_specs=[vmem] * len(outs),
        compiler_params=pltpu.CompilerParams(vmem_limit_bytes=VMEM),
        name="finish_tiled" if tiles is not None else "finish",
    )(*own, *other)


def time_product(sigma, panel, free, tiled):
    zl = lax.axis_index(ZL)
    column = lax.axis_index("l")
    per = lax.axis_size("x")
    rows = jnp.stack([zl, lax.bitwise_xor(zl, 2)])
    own_blocks = column * per + rows
    other_blocks = (1 - column) * per + rows
    slabs = sigma.shape[0] // CHUNKS
    mine = [sigma[i * slabs : (i + 1) * slabs] for i in range(CHUNKS)]
    swapped = [lax.ppermute(x, ZL, [(0, 2), (1, 3), (2, 0), (3, 1)]) for x in mine]
    own, other = [], []
    for i, (left, right) in enumerate(zip(mine, swapped)):
        if own:
            right, own[-1], _ = lax.optimization_barrier((right, own[-1], part))
        pair = (left, right)
        part = product(pair, panel, other_blocks)
        other.append(lax.ppermute(part, ZL, [(0, 1), (1, 0), (2, 3), (3, 2)]))
        own.append(product(pair, panel, own_blocks, free, i))
    return finish(own, other, sigma.shape if tiled else None)


def pack(free, greater):
    return jnp.concatenate([free, greater], axis=0).swapaxes(0, 1)


def exchange(x):
    return lax.all_to_all(x, ("zh", "y"), 0, 0, tiled=True)


def body(g_free, g_greater_t, momentum_map, weights):
    momenta = momentum_map.shape[0]
    free, greater = g_free[:, 0], g_greater_t[:, 0]
    tile_rows, tile_cols = free.shape[1:]
    slabs = (2, momenta, tile_rows // momenta, tile_cols)
    weights = weights.reshape(-1, 1, tile_cols)

    green = free
    field = exchange(pack(free.reshape(slabs), greater.reshape(slabs)))
    mirror = None
    for sweep in range(ITERS):
        panel = lax.all_gather(green, ("l", "x", "core"))
        panel = pltpu.with_memory_space_constraint(panel, pltpu.HBM)
        if mirror is None:
            sigma, mirror = self_energy(momentum_map, weights, field)
        else:
            sigma = self_energy(momentum_map, weights, field, mirror)
        sigma = exchange(sigma)
        if sweep == ITERS - 1:
            return time_product(sigma, panel, free, False)[0][:, None]
        green, tiles = time_product(sigma, panel, free, True)
        field = exchange(tiles)


def solution(mesh):
    fine = Mesh(mesh.devices.reshape(3, 8, 2, 2, 4, 2), ("zh", "y", "h", "l", "x", "core"))
    spec = P(None, ("zh", "y"), ("x", "core"), ZL)
    return jax.shard_map(
        body, mesh=fine, in_specs=(spec, spec, P(), P()), out_specs=spec, check_vma=False
    )
```

```python
import math

import jax
import jax.numpy as jnp
from jax import lax
from jax.experimental import pallas as pl
from jax.experimental.pallas import tpu as pltpu
from jax.sharding import Mesh, PartitionSpec as P

LY = 4
ITERS = 2


CHUNKS = 2
VMEM = 24 * 1024 * 1024

LANES = 128
ROOT3_2 = math.sqrt(3.0) / 2.0


def c_add(a, b):
    return (a[0] + b[0], a[1] + b[1])


def c_sub(a, b):
    return (a[0] - b[0], a[1] - b[1])


def c_turn(a, sign):
    return (-a[1], a[0]) if sign > 0 else (a[1], -a[0])


def dft3(x0, x1, x2, sign):
    u = c_add(x1, x2)
    v = c_sub(x1, x2)
    m = (x0[0] - 0.5 * u[0], x0[1] - 0.5 * u[1])
    n = c_turn((ROOT3_2 * v[0], ROOT3_2 * v[1]), sign)
    return c_add(x0, u), c_add(m, n), c_sub(m, n)


def dft4(x, sign):
    t0, t1 = c_add(x[0], x[2]), c_sub(x[0], x[2])
    t2, t3 = c_add(x[1], x[3]), c_turn(c_sub(x[1], x[3]), sign)
    return [c_add(t0, t2), c_add(t1, t3), c_sub(t0, t2), c_sub(t1, t3)]


def dft6(x, sign):
    b = [c_add(x[m], x[m + 3]) for m in range(3)]
    c = [c_sub(x[m], x[m + 3]) for m in range(3)]
    even = dft3(b[0], b[1], b[2], sign)
    odd = dft3(c[0], (-c[1][0], -c[1][1]), c[2], sign)
    return [even[0], odd[2], even[1], odd[0], even[2], odd[1]]


def lattice_transform(x, sign):
    rows = [[None] * 6 for _ in range(4)]
    for across in range(6):
        column = dft4([x[6 * down + across] for down in range(4)], sign)
        for down in range(4):
            rows[down][across] = column[down]
    out = []
    for down in range(4):
        out.extend(dft6(rows[down], sign))
    return out


def self_energy_kernel(first, map_ref, weights_ref, field_ref, *refs):
    if first:
        sigma_ref, mirror_ref, where_ref = refs
    else:
        mirror_ref, sigma_ref, where_ref = refs
    momenta = field_ref.shape[0]
    for k in range(momenta):
        where_ref[map_ref[k]] = k
    spot = [where_ref[q] for q in range(momenta)]
    zl = lax.axis_index("zl")
    for lane in range(0, field_ref.shape[3], LANES):
        cut = pl.ds(lane, LANES)
        if first:
            mirror = lattice_transform(
                [(field_ref[k, 2, :, cut], field_ref[k, 3, :, cut]) for k in spot], -1
            )
            scale = 1.0 / (momenta * momenta)
            for r in range(momenta):
                mirror_ref[r, 0, :, cut] = mirror[r][0] * scale
                mirror_ref[r, 1, :, cut] = mirror[r][1] * scale
        space = lattice_transform(
            [(field_ref[k, 0, :, cut], field_ref[k, 1, :, cut]) for k in spot], 1
        )
        source = []
        for r in range(momenta):
            re, im = space[r]
            sq_re = re * re - im * im
            sq_im = 2.0 * re * im
            m_re, m_im = mirror_ref[r, 0, :, cut], mirror_ref[r, 1, :, cut]
            source.append((sq_re * m_re - sq_im * m_im, sq_re * m_im + sq_im * m_re))
        sigma = lattice_transform(source, -1)
        w = weights_ref[zl, :, cut]
        for q in range(momenta):
            sigma_ref[spot[q], 0, :, cut] = sigma[q][0] * w
            sigma_ref[spot[q], 1, :, cut] = sigma[q][1] * w


def self_energy(momentum_map, weights, field, mirror=None):
    first = mirror is None
    momenta, _, rows, cols = field.shape
    shape = jax.ShapeDtypeStruct((momenta, 2, rows, cols), jnp.float32)
    smem = pl.BlockSpec(memory_space=pltpu.SMEM)
    vmem = pl.BlockSpec(memory_space=pltpu.VMEM)
    ins = [momentum_map, weights, field] + ([] if first else [mirror])
    return pl.pallas_call(
        lambda *refs: self_energy_kernel(first, *refs),
        out_shape=(shape, shape) if first else shape,
        in_specs=[smem] + [vmem] * (len(ins) - 1),
        out_specs=(vmem, vmem) if first else vmem,
        scratch_shapes=[pltpu.SMEM((momenta,), jnp.int32)],
        compiler_params=pltpu.CompilerParams(vmem_limit_bytes=VMEM),
        name="self_energy_first" if first else "self_energy_next",
    )(*ins)


def split_left(x):
    hi = x.astype(jnp.bfloat16)
    lo = (x - hi.astype(jnp.float32)).astype(jnp.bfloat16)
    return jnp.concatenate([hi, lo, hi], axis=1)


def split_right(x):
    hi = x.astype(jnp.bfloat16)
    lo = (x - hi.astype(jnp.float32)).astype(jnp.bfloat16)
    return jnp.concatenate([hi, hi, lo], axis=0)


def mul(a, b):
    return jnp.dot(split_left(a), split_right(b), preferred_element_type=jnp.float32)


def product_kernel(counts, tiled, n_done, blocks_ref, *refs):
    terms = []
    for n in counts:
        terms.append((refs[:n], refs[n]))
        refs = refs[n + 1 :]
    base_ref, done, outs = refs[0], refs[1 : 1 + n_done], refs[1 + n_done :]

    def flat(x):
        return x.reshape(x.shape[0] * x.shape[1], x.shape[2])

    def left(holders, j):
        x = holders[0][:, j]
        for ref in holders[1:]:
            x = x + ref[:, j]
        return flat(x)

    re, im = base_ref[0], base_ref[1]
    for holders, panel_ref in terms:
        s_re, s_im = left(holders, 0), left(holders, 1)
        g_re, g_im = flat(panel_ref[:, 0]), flat(panel_ref[:, 1])
        one = mul(s_re, g_re)
        two = mul(s_im, g_im)
        three = mul(s_re + s_im, g_re + g_im)
        re, im = re + (one - two), im + (three - one - two)
    rows = re.shape[0]
    for i, pair in enumerate([(ref[0], ref[1]) for ref in done] + [(re, im)]):
        for j in range(2):
            outs[0][j, i * rows : (i + 1) * rows] = pair[j]
            if tiled:
                slabs = outs[1].shape[0] // (n_done + 1)
                outs[1][i * slabs : (i + 1) * slabs, j] = pair[j].reshape(
                    (slabs,) + outs[1].shape[2:]
                )


def product(terms, panel, base, chunk=0, done=(), tiled=False):
    slabs, _, high, cols = terms[0][0][0].shape
    rows = slabs * high
    per = cols // panel.shape[2]
    full = lambda shape: pl.BlockSpec(shape, lambda i, b: (0,) * len(shape))
    in_specs, ins = [], []
    for j, (lefts, _) in enumerate(terms):
        in_specs += [full(x.shape) for x in lefts]
        in_specs.append(
            pl.BlockSpec((per,) + panel.shape[1:], lambda i, b, j=j: (b[j], 0, 0, 0))
        )
        ins += list(lefts) + [panel]
    at = chunk if base.shape[1] != rows else 0
    in_specs.append(pl.BlockSpec((2, rows, cols), lambda i, b: (0, at, 0)))
    in_specs += [full(x.shape) for x in done]
    outs = [jax.ShapeDtypeStruct((2, rows * (1 + len(done)), cols), jnp.float32)]
    if tiled:
        outs.append(jax.ShapeDtypeStruct((slabs * (1 + len(done)), 2, high, cols), jnp.float32))
    counts = [len(lefts) for lefts, _ in terms]
    return pl.pallas_call(
        lambda *refs: product_kernel(counts, tiled, len(done), *refs),
        out_shape=outs,
        grid_spec=pltpu.PrefetchScalarGridSpec(
            num_scalar_prefetch=1,
            grid=(1,),
            in_specs=in_specs,
            out_specs=[full(o.shape) for o in outs],
        ),
        compiler_params=pltpu.CompilerParams(vmem_limit_bytes=VMEM),
        name="product_last" if done else "product",
    )(jnp.stack([block for _, block in terms]), *ins, base, *done)


def time_product(sigma, panel, free, tiled):
    zl = lax.axis_index("zl")
    low = zl < 2
    near_block = lax.bitwise_xor(zl, 1)
    two_block, far_block = jnp.where(low, 2, 1), jnp.where(low, 3, 0)
    slabs = sigma.shape[0] // CHUNKS
    mine = [sigma[i * slabs : (i + 1) * slabs] for i in range(CHUNKS)]
    across, middle, outwards = [(0, 1), (1, 0), (2, 3), (3, 2)], [(1, 2), (2, 1)], [(1, 0), (2, 3)]
    send = lambda xs, pairs: [lax.ppermute(x, "zl", pairs) for x in xs]
    mid = send(mine, middle)
    near = send(mine, across)
    end_two = send(mid, outwards)
    mid_far = send(near, middle)
    end_far = send(mid_far, outwards)
    totals = [
        product([([mine[i]], zl), ([near[i]], near_block)], panel, free, i)[0]
        for i in range(CHUNKS)
    ]
    totals = [
        product([([mid[i], end_two[i]], two_block)], panel, totals[i])[0] for i in range(CHUNKS)
    ]
    done = []
    for i in range(CHUNKS):
        last = i == CHUNKS - 1
        res = product(
            [([mid_far[i], end_far[i]], far_block)],
            panel,
            totals[i],
            done=done if last else (),
            tiled=tiled and last,
        )
        done.append(res[0])
    return res


def pack(free, greater):
    return jnp.concatenate([free, greater], axis=0).swapaxes(0, 1)


def exchange(x):
    return lax.all_to_all(x, ("zh", "y"), 0, 0, tiled=True)


def body(g_free, g_greater_t, momentum_map, weights):
    momenta = momentum_map.shape[0]
    free, greater = g_free[:, 0], g_greater_t[:, 0]
    tile_rows, tile_cols = free.shape[1:]
    slabs = (2, momenta, tile_rows // momenta, tile_cols)
    weights = weights.reshape(-1, 1, tile_cols)

    green = free
    field = exchange(pack(free.reshape(slabs), greater.reshape(slabs)))
    mirror = None
    for sweep in range(ITERS):
        panel = lax.all_gather(green, ("x", "core"))
        panel = pltpu.with_memory_space_constraint(panel, pltpu.HBM)
        if mirror is None:
            sigma, mirror = self_energy(momentum_map, weights, field)
        else:
            sigma = self_energy(momentum_map, weights, field, mirror)
        sigma = exchange(sigma)
        if sweep == ITERS - 1:
            return time_product(sigma, panel, free, False)[0][:, None]
        green, tiles = time_product(sigma, panel, free, True)
        field = exchange(tiles)


def solution(mesh):
    fine = Mesh(mesh.devices.reshape(3, 8, 4, 4, 2), ("zh", "y", "zl", "x", "core"))
    spec = P(None, ("zh", "y"), ("x", "core"), "zl")
    return jax.shard_map(
        body, mesh=fine, in_specs=(spec, spec, P(), P()), out_specs=spec, check_vma=False
    )
```

```python
import math

import jax
import jax.numpy as jnp
from jax import lax
from jax.experimental import pallas as pl
from jax.experimental.pallas import tpu as pltpu
from jax.sharding import Mesh, PartitionSpec as P


ITERS = 2


CHUNKS = 2
VMEM = 24 * 1024 * 1024

LANES = 128
ROOT3_2 = math.sqrt(3.0) / 2.0


def c_add(a, b):
    return (a[0] + b[0], a[1] + b[1])


def c_sub(a, b):
    return (a[0] - b[0], a[1] - b[1])


def c_turn(a, sign):
    return (-a[1], a[0]) if sign > 0 else (a[1], -a[0])


def dft3(x0, x1, x2, sign):
    u = c_add(x1, x2)
    v = c_sub(x1, x2)
    m = (x0[0] - 0.5 * u[0], x0[1] - 0.5 * u[1])
    n = c_turn((ROOT3_2 * v[0], ROOT3_2 * v[1]), sign)
    return c_add(x0, u), c_add(m, n), c_sub(m, n)


def dft4(x, sign):
    t0, t1 = c_add(x[0], x[2]), c_sub(x[0], x[2])
    t2, t3 = c_add(x[1], x[3]), c_turn(c_sub(x[1], x[3]), sign)
    return [c_add(t0, t2), c_add(t1, t3), c_sub(t0, t2), c_sub(t1, t3)]


def dft6(x, sign):
    b = [c_add(x[m], x[m + 3]) for m in range(3)]
    c = [c_sub(x[m], x[m + 3]) for m in range(3)]
    even = dft3(b[0], b[1], b[2], sign)
    odd = dft3(c[0], (-c[1][0], -c[1][1]), c[2], sign)
    return [even[0], odd[2], even[1], odd[0], even[2], odd[1]]


def lattice_transform(x, sign):
    rows = [[None] * 6 for _ in range(4)]
    for across in range(6):
        column = dft4([x[6 * down + across] for down in range(4)], sign)
        for down in range(4):
            rows[down][across] = column[down]
    out = []
    for down in range(4):
        out.extend(dft6(rows[down], sign))
    return out


def self_energy_kernel(first, map_ref, weights_ref, field_ref, *refs):
    if first:
        sigma_ref, mirror_ref, where_ref = refs
    else:
        mirror_ref, sigma_ref, where_ref = refs
    momenta = field_ref.shape[0]
    for k in range(momenta):
        where_ref[map_ref[k]] = k
    spot = [where_ref[q] for q in range(momenta)]
    zl = lax.axis_index("zl")
    for lane in range(0, field_ref.shape[3], LANES):
        cut = pl.ds(lane, LANES)
        if first:
            mirror = lattice_transform(
                [(field_ref[k, 2, :, cut], field_ref[k, 3, :, cut]) for k in spot], -1
            )
            scale = 1.0 / (momenta * momenta)
            for r in range(momenta):
                mirror_ref[r, 0, :, cut] = mirror[r][0] * scale
                mirror_ref[r, 1, :, cut] = mirror[r][1] * scale
        space = lattice_transform(
            [(field_ref[k, 0, :, cut], field_ref[k, 1, :, cut]) for k in spot], 1
        )
        source = []
        for r in range(momenta):
            re, im = space[r]
            sq_re = re * re - im * im
            sq_im = 2.0 * re * im
            m_re, m_im = mirror_ref[r, 0, :, cut], mirror_ref[r, 1, :, cut]
            source.append((sq_re * m_re - sq_im * m_im, sq_re * m_im + sq_im * m_re))
        sigma = lattice_transform(source, -1)
        w = weights_ref[zl, :, cut]
        for q in range(momenta):
            sigma_ref[spot[q], 0, :, cut] = sigma[q][0] * w
            sigma_ref[spot[q], 1, :, cut] = sigma[q][1] * w


def self_energy(momentum_map, weights, field, mirror=None):
    first = mirror is None
    momenta, _, rows, cols = field.shape
    shape = jax.ShapeDtypeStruct((momenta, 2, rows, cols), jnp.float32)
    smem = pl.BlockSpec(memory_space=pltpu.SMEM)
    vmem = pl.BlockSpec(memory_space=pltpu.VMEM)
    ins = [momentum_map, weights, field] + ([] if first else [mirror])
    return pl.pallas_call(
        lambda *refs: self_energy_kernel(first, *refs),
        out_shape=(shape, shape) if first else shape,
        in_specs=[smem] + [vmem] * (len(ins) - 1),
        out_specs=(vmem, vmem) if first else vmem,
        scratch_shapes=[pltpu.SMEM((momenta,), jnp.int32)],
        compiler_params=pltpu.CompilerParams(vmem_limit_bytes=VMEM),
        name="self_energy_first" if first else "self_energy_next",
    )(*ins)


def split_left(x):
    hi = x.astype(jnp.bfloat16)
    lo = (x - hi.astype(jnp.float32)).astype(jnp.bfloat16)
    return jnp.concatenate([hi, lo, hi], axis=1)


def split_right(x):
    hi = x.astype(jnp.bfloat16)
    lo = (x - hi.astype(jnp.float32)).astype(jnp.bfloat16)
    return jnp.concatenate([hi, hi, lo], axis=0)


def mul(a, b):
    return jnp.dot(split_left(a), split_right(b), preferred_element_type=jnp.float32)


def product_kernel(counts, tiled, n_done, blocks_ref, *refs):
    terms = []
    for n in counts:
        terms.append((refs[:n], refs[n]))
        refs = refs[n + 1 :]
    base_ref, done, outs = refs[0], refs[1 : 1 + n_done], refs[1 + n_done :]

    def flat(x):
        return x.reshape(x.shape[0] * x.shape[1], x.shape[2])

    def left(holders, j):
        x = holders[0][:, j]
        for ref in holders[1:]:
            x = x + ref[:, j]
        return flat(x)

    re, im = base_ref[0], base_ref[1]
    for holders, panel_ref in terms:
        s_re, s_im = left(holders, 0), left(holders, 1)
        g_re, g_im = flat(panel_ref[:, 0]), flat(panel_ref[:, 1])
        one = mul(s_re, g_re)
        two = mul(s_im, g_im)
        three = mul(s_re + s_im, g_re + g_im)
        re, im = re + (one - two), im + (three - one - two)
    rows = re.shape[0]
    for i, pair in enumerate([(ref[0], ref[1]) for ref in done] + [(re, im)]):
        for j in range(2):
            outs[0][j, i * rows : (i + 1) * rows] = pair[j]
            if tiled:
                slabs = outs[1].shape[0] // (n_done + 1)
                outs[1][i * slabs : (i + 1) * slabs, j] = pair[j].reshape(
                    (slabs,) + outs[1].shape[2:]
                )


def product(terms, panel, base, chunk=0, done=(), tiled=False):
    slabs, _, high, cols = terms[0][0][0].shape
    rows = slabs * high
    per = cols // panel.shape[2]
    full = lambda shape: pl.BlockSpec(shape, lambda i, b: (0,) * len(shape))
    in_specs, ins = [], []
    for j, (lefts, _) in enumerate(terms):
        in_specs += [full(x.shape) for x in lefts]
        in_specs.append(
            pl.BlockSpec((per,) + panel.shape[1:], lambda i, b, j=j: (b[j], 0, 0, 0))
        )
        ins += list(lefts) + [panel]
    at = chunk if base.shape[1] != rows else 0
    in_specs.append(pl.BlockSpec((2, rows, cols), lambda i, b: (0, at, 0)))
    in_specs += [full(x.shape) for x in done]
    outs = [jax.ShapeDtypeStruct((2, rows * (1 + len(done)), cols), jnp.float32)]
    if tiled:
        outs.append(jax.ShapeDtypeStruct((slabs * (1 + len(done)), 2, high, cols), jnp.float32))
    counts = [len(lefts) for lefts, _ in terms]
    return pl.pallas_call(
        lambda *refs: product_kernel(counts, tiled, len(done), *refs),
        out_shape=outs,
        grid_spec=pltpu.PrefetchScalarGridSpec(
            num_scalar_prefetch=1,
            grid=(1,),
            in_specs=in_specs,
            out_specs=[full(o.shape) for o in outs],
        ),
        compiler_params=pltpu.CompilerParams(vmem_limit_bytes=VMEM),
        name="product_last" if done else "product",
    )(jnp.stack([block for _, block in terms]), *ins, base, *done)


def time_product(sigma, panel, free, tiled):
    zl = lax.axis_index("zl")
    low = zl < 2
    near_block = lax.bitwise_xor(zl, 1)
    two_block, far_block = jnp.where(low, 2, 1), jnp.where(low, 3, 0)
    slabs = sigma.shape[0] // CHUNKS
    mine = [sigma[i * slabs : (i + 1) * slabs] for i in range(CHUNKS)]
    across, middle, outwards = [(0, 1), (1, 0), (2, 3), (3, 2)], [(1, 2), (2, 1)], [(1, 0), (2, 3)]

    def send(xs, pairs):
        out = []
        for x in xs:
            out.append(lax.ppermute(x, "zl", pairs))
        return out

    mid = send(mine, middle)
    near = send(mine, across)
    end_two = send(mid, outwards)
    mid_far = send(near, middle)
    end_far = send(mid_far, outwards)
    totals = []
    for i in range(CHUNKS):
        terms = [([mine[i]], zl), ([near[i]], near_block)]
        totals.append(product(terms, panel, free, i)[0])
    totals = [
        product([([mid[i], end_two[i]], two_block)], panel, totals[i])[0] for i in range(CHUNKS)
    ]
    done = []
    for i in range(CHUNKS):
        last = i == CHUNKS - 1
        res = product(
            [([mid_far[i], end_far[i]], far_block)],
            panel,
            totals[i],
            done=done if last else (),
            tiled=tiled and last,
        )
        done.append(res[0])
    return res


def pack(free, greater):
    return jnp.concatenate([free, greater], axis=0).swapaxes(0, 1)


def exchange(x):
    return lax.all_to_all(x, ("zh", "y"), 0, 0, tiled=True)


def body(g_free, g_greater_t, momentum_map, weights):
    momenta = momentum_map.shape[0]
    free, greater = g_free[:, 0], g_greater_t[:, 0]
    tile_rows, tile_cols = free.shape[1:]
    slabs = (2, momenta, tile_rows // momenta, tile_cols)
    weights = weights.reshape(-1, 1, tile_cols)

    green = free
    field = exchange(pack(free.reshape(slabs), greater.reshape(slabs)))
    mirror = None
    for sweep in range(ITERS):
        panel = lax.all_gather(green, ("x", "core"))
        panel = pltpu.with_memory_space_constraint(panel, pltpu.HBM)
        if mirror is None:
            sigma, mirror = self_energy(momentum_map, weights, field)
        else:
            sigma = self_energy(momentum_map, weights, field, mirror)
        sigma = exchange(sigma)
        if sweep == ITERS - 1:
            return time_product(sigma, panel, free, False)[0][:, None]
        green, tiles = time_product(sigma, panel, free, True)
        field = exchange(tiles)


def solution(mesh):
    fine = Mesh(mesh.devices.reshape(3, 8, 4, 4, 2), ("zh", "y", "zl", "x", "core"))
    spec = P(None, ("zh", "y"), ("x", "core"), "zl")
    return jax.shard_map(
        body, mesh=fine, in_specs=(spec, spec, P(), P()), out_specs=spec, check_vma=False
    )
```

```python
import math

import jax
import jax.numpy as jnp
from jax import lax
from jax.experimental import pallas as pl
from jax.experimental.pallas import tpu as pltpu
from jax.sharding import Mesh, PartitionSpec as P


ITERS = 2


CHUNKS = 2
VMEM = 16 * 1024 * 1024

LANES = 128
ROOT3_2 = math.sqrt(3.0) / 2.0


def c_add(a, b):
    return (a[0] + b[0], a[1] + b[1])


def c_sub(a, b):
    return (a[0] - b[0], a[1] - b[1])


def c_turn(a, sign):
    return (-a[1], a[0]) if sign > 0 else (a[1], -a[0])


def dft3(x0, x1, x2, sign):
    u = c_add(x1, x2)
    v = c_sub(x1, x2)
    m = (x0[0] - 0.5 * u[0], x0[1] - 0.5 * u[1])
    n = c_turn((ROOT3_2 * v[0], ROOT3_2 * v[1]), sign)
    return c_add(x0, u), c_add(m, n), c_sub(m, n)


def dft4(x, sign):
    t0, t1 = c_add(x[0], x[2]), c_sub(x[0], x[2])
    t2, t3 = c_add(x[1], x[3]), c_turn(c_sub(x[1], x[3]), sign)
    return [c_add(t0, t2), c_add(t1, t3), c_sub(t0, t2), c_sub(t1, t3)]


def dft6(x, sign):
    b = [c_add(x[m], x[m + 3]) for m in range(3)]
    c = [c_sub(x[m], x[m + 3]) for m in range(3)]
    even = dft3(b[0], b[1], b[2], sign)
    odd = dft3(c[0], (-c[1][0], -c[1][1]), c[2], sign)
    return [even[0], odd[2], even[1], odd[0], even[2], odd[1]]


def lattice_transform(x, sign):
    rows = [[None] * 6 for _ in range(4)]
    for across in range(6):
        column = dft4([x[6 * down + across] for down in range(4)], sign)
        for down in range(4):
            rows[down][across] = column[down]
    out = []
    for down in range(4):
        out.extend(dft6(rows[down], sign))
    return out


def self_energy_kernel(first, map_ref, weights_ref, field_ref, *refs):
    if first:
        sigma_ref, mirror_ref, where_ref = refs
    else:
        mirror_ref, sigma_ref, where_ref = refs
    momenta = field_ref.shape[0]
    ny, nz = lax.axis_size("y"), lax.axis_size("zh")
    for k in range(momenta):
        where_ref[map_ref[k]] = k % ny * nz + k // ny
    spot = [where_ref[q] for q in range(momenta)]
    zl = lax.axis_index("zl")
    for lane in range(0, field_ref.shape[3], LANES):
        cut = pl.ds(lane, LANES)
        if first:
            mirror = lattice_transform(
                [(field_ref[k, 2, :, cut], field_ref[k, 3, :, cut]) for k in spot], -1
            )
            scale = 1.0 / (momenta * momenta)
            for r in range(momenta):
                mirror_ref[r, 0, :, cut] = mirror[r][0] * scale
                mirror_ref[r, 1, :, cut] = mirror[r][1] * scale
        space = lattice_transform(
            [(field_ref[k, 0, :, cut], field_ref[k, 1, :, cut]) for k in spot], 1
        )
        source = []
        for r in range(momenta):
            re, im = space[r]
            sq_re = re * re - im * im
            sq_im = 2.0 * re * im
            m_re, m_im = mirror_ref[r, 0, :, cut], mirror_ref[r, 1, :, cut]
            source.append((sq_re * m_re - sq_im * m_im, sq_re * m_im + sq_im * m_re))
        sigma = lattice_transform(source, -1)
        w = weights_ref[zl, :, cut]
        for q in range(momenta):
            sigma_ref[spot[q], 0, :, cut] = sigma[q][0] * w
            sigma_ref[spot[q], 1, :, cut] = sigma[q][1] * w


def self_energy(momentum_map, weights, field, mirror=None):
    first = mirror is None
    momenta, _, rows, cols = field.shape
    shape = jax.ShapeDtypeStruct((momenta, 2, rows, cols), jnp.float32)
    smem = pl.BlockSpec(memory_space=pltpu.SMEM)
    vmem = pl.BlockSpec(memory_space=pltpu.VMEM)
    ins = [momentum_map, weights, field] + ([] if first else [mirror])
    return pl.pallas_call(
        lambda *refs: self_energy_kernel(first, *refs),
        out_shape=(shape, shape) if first else shape,
        in_specs=[smem] + [vmem] * (len(ins) - 1),
        out_specs=(vmem, vmem) if first else vmem,
        scratch_shapes=[pltpu.SMEM((momenta,), jnp.int32)],
        compiler_params=pltpu.CompilerParams(vmem_limit_bytes=VMEM),
        name="self_energy_first" if first else "self_energy_next",
    )(*ins)


def split_left(x):
    hi = x.astype(jnp.bfloat16)
    lo = (x - hi.astype(jnp.float32)).astype(jnp.bfloat16)
    return jnp.concatenate([hi, lo, hi], axis=1)


def split_right(x):
    hi = x.astype(jnp.bfloat16)
    lo = (x - hi.astype(jnp.float32)).astype(jnp.bfloat16)
    return jnp.concatenate([hi, hi, lo], axis=0)


def mul(a, b):
    return jnp.dot(split_left(a), split_right(b), preferred_element_type=jnp.float32)


def product_kernel(counts, tiled, n_done, blocks_ref, *refs):
    terms = []
    for n in counts:
        terms.append((refs[:n], refs[n]))
        refs = refs[n + 1 :]
    base_ref, done, outs = refs[0], refs[1 : 1 + n_done], refs[1 + n_done :]

    def flat(x):
        return x.reshape(x.shape[0] * x.shape[1], x.shape[2])

    def left(holders, j):
        x = holders[0][:, j]
        for ref in holders[1:]:
            x = x + ref[:, j]
        return flat(x)

    re, im = base_ref[0], base_ref[1]
    for holders, panel_ref in terms:
        s_re, s_im = left(holders, 0), left(holders, 1)
        g_re, g_im = flat(panel_ref[:, 0]), flat(panel_ref[:, 1])
        one = mul(s_re, g_re)
        two = mul(s_im, g_im)
        three = mul(s_re + s_im, g_re + g_im)
        re, im = re + (one - two), im + (three - one - two)
    rows = re.shape[0]
    for i, pair in enumerate([(ref[0], ref[1]) for ref in done] + [(re, im)]):
        for j in range(2):
            outs[0][j, i * rows : (i + 1) * rows] = pair[j]
            if tiled:
                slabs = outs[1].shape[0] // (n_done + 1)
                outs[1][i * slabs : (i + 1) * slabs, j] = pair[j].reshape(
                    (slabs,) + outs[1].shape[2:]
                )


def product(terms, panel, base, chunk=0, done=(), tiled=False):
    slabs, _, high, cols = terms[0][0][0].shape
    rows = slabs * high
    per = cols // panel.shape[2]
    full = lambda shape: pl.BlockSpec(shape, lambda i, b: (0,) * len(shape))
    in_specs, ins = [], []
    for j, (lefts, _) in enumerate(terms):
        in_specs += [full(x.shape) for x in lefts]
        in_specs.append(
            pl.BlockSpec((per,) + panel.shape[1:], lambda i, b, j=j: (b[j], 0, 0, 0))
        )
        ins += list(lefts) + [panel]
    at = chunk if base.shape[1] != rows else 0
    in_specs.append(pl.BlockSpec((2, rows, cols), lambda i, b: (0, at, 0)))
    in_specs += [full(x.shape) for x in done]
    outs = [jax.ShapeDtypeStruct((2, rows * (1 + len(done)), cols), jnp.float32)]
    if tiled:
        outs.append(jax.ShapeDtypeStruct((slabs * (1 + len(done)), 2, high, cols), jnp.float32))
    counts = [len(lefts) for lefts, _ in terms]
    return pl.pallas_call(
        lambda *refs: product_kernel(counts, tiled, len(done), *refs),
        out_shape=outs,
        grid_spec=pltpu.PrefetchScalarGridSpec(
            num_scalar_prefetch=1,
            grid=(1,),
            in_specs=in_specs,
            out_specs=[full(o.shape) for o in outs],
        ),
        compiler_params=pltpu.CompilerParams(vmem_limit_bytes=VMEM),
        name="product_last" if done else "product",
    )(jnp.stack([block for _, block in terms]), *ins, base, *done)


def time_product(sigma, panel, free, tiled):
    zl = lax.axis_index("zl")
    low = zl < 2
    near_block = lax.bitwise_xor(zl, 1)
    two_block, far_block = jnp.where(low, 2, 1), jnp.where(low, 3, 0)
    slabs = sigma.shape[0] // CHUNKS
    mine = [sigma[i * slabs : (i + 1) * slabs] for i in range(CHUNKS)]
    across, middle, outwards = [(0, 1), (1, 0), (2, 3), (3, 2)], [(1, 2), (2, 1)], [(1, 0), (2, 3)]

    def send(xs, pairs):
        out = []
        for x in xs:
            out.append(lax.ppermute(x, "zl", pairs))
        return out

    mid = send(mine, middle)
    near = send(mine, across)
    end_two = send(mid, outwards)
    mid_far = send(near, middle)
    end_far = send(mid_far, outwards)
    totals = []
    for i in range(CHUNKS):
        terms = [([mine[i]], zl), ([near[i]], near_block)]
        totals.append(product(terms, panel, free, i)[0])
    totals = [
        product([([mid[i], end_two[i]], two_block)], panel, totals[i])[0] for i in range(CHUNKS)
    ]
    done = []
    for i in range(CHUNKS):
        last = i == CHUNKS - 1
        res = product(
            [([mid_far[i], end_far[i]], far_block)],
            panel,
            totals[i],
            done=done if last else (),
            tiled=tiled and last,
        )
        done.append(res[0])
    return res


def pack(free, greater):
    return jnp.concatenate([free, greater], axis=0).swapaxes(0, 1)


def exchange(x):
    return lax.all_to_all(x, ("y", "zh"), 0, 0, tiled=True)


def body(g_free, g_greater_t, momentum_map, weights):
    momenta = momentum_map.shape[0]
    free, greater = g_free[:, 0], g_greater_t[:, 0]
    tile_rows, tile_cols = free.shape[1:]
    slabs = (2, momenta, tile_rows // momenta, tile_cols)
    weights = weights.reshape(-1, 1, tile_cols)

    green = free
    field = exchange(pack(free.reshape(slabs), greater.reshape(slabs)))
    mirror = None
    for sweep in range(ITERS):
        panel = lax.all_gather(green, ("x", "core"))
        panel = pltpu.with_memory_space_constraint(panel, pltpu.HBM)
        if mirror is None:
            sigma, mirror = self_energy(momentum_map, weights, field)
        else:
            sigma = self_energy(momentum_map, weights, field, mirror)
        sigma = exchange(sigma)
        if sweep == ITERS - 1:
            return time_product(sigma, panel, free, False)[0][:, None]
        green, tiles = time_product(sigma, panel, free, True)
        field = exchange(tiles)


def solution(mesh):
    fine = Mesh(mesh.devices.reshape(3, 8, 4, 4, 2), ("zh", "y", "zl", "x", "core"))
    spec = P(None, ("zh", "y"), ("x", "core"), "zl")
    return jax.shard_map(
        body, mesh=fine, in_specs=(spec, spec, P(), P()), out_specs=spec, check_vma=False
    )
```

```python
import math

import jax
import jax.numpy as jnp
from jax import lax
from jax.experimental import pallas as pl
from jax.experimental.pallas import tpu as pltpu
from jax.sharding import Mesh, PartitionSpec as P


ITERS = 2


CHUNKS = 3
VMEM = 16 * 1024 * 1024

LANES = 128
ROOT3_2 = math.sqrt(3.0) / 2.0


def c_add(a, b):
    return (a[0] + b[0], a[1] + b[1])


def c_sub(a, b):
    return (a[0] - b[0], a[1] - b[1])


def c_turn(a, sign):
    return (-a[1], a[0]) if sign > 0 else (a[1], -a[0])


def dft3(x0, x1, x2, sign):
    u = c_add(x1, x2)
    v = c_sub(x1, x2)
    m = (x0[0] - 0.5 * u[0], x0[1] - 0.5 * u[1])
    n = c_turn((ROOT3_2 * v[0], ROOT3_2 * v[1]), sign)
    return c_add(x0, u), c_add(m, n), c_sub(m, n)


def dft4(x, sign):
    t0, t1 = c_add(x[0], x[2]), c_sub(x[0], x[2])
    t2, t3 = c_add(x[1], x[3]), c_turn(c_sub(x[1], x[3]), sign)
    return [c_add(t0, t2), c_add(t1, t3), c_sub(t0, t2), c_sub(t1, t3)]


def dft6(x, sign):
    b = [c_add(x[m], x[m + 3]) for m in range(3)]
    c = [c_sub(x[m], x[m + 3]) for m in range(3)]
    even = dft3(b[0], b[1], b[2], sign)
    odd = dft3(c[0], (-c[1][0], -c[1][1]), c[2], sign)
    return [even[0], odd[2], even[1], odd[0], even[2], odd[1]]


def lattice_transform(x, sign):
    rows = [[None] * 6 for _ in range(4)]
    for across in range(6):
        column = dft4([x[6 * down + across] for down in range(4)], sign)
        for down in range(4):
            rows[down][across] = column[down]
    out = []
    for down in range(4):
        out.extend(dft6(rows[down], sign))
    return out


def self_energy_kernel(first, map_ref, weights_ref, field_ref, *refs):
    if first:
        sigma_ref, mirror_ref, where_ref = refs
    else:
        mirror_ref, sigma_ref, where_ref = refs
    momenta = field_ref.shape[0]
    ny, nz = lax.axis_size("y"), lax.axis_size("zh")
    for k in range(momenta):
        where_ref[map_ref[k]] = k % ny * nz + k // ny
    spot = [where_ref[q] for q in range(momenta)]
    zl = lax.axis_index("zl")
    for lane in range(0, field_ref.shape[3], LANES):
        cut = pl.ds(lane, LANES)
        if first:
            mirror = lattice_transform(
                [(field_ref[k, 2, :, cut], field_ref[k, 3, :, cut]) for k in spot], -1
            )
            scale = 1.0 / (momenta * momenta)
            for r in range(momenta):
                mirror_ref[r, 0, :, cut] = mirror[r][0] * scale
                mirror_ref[r, 1, :, cut] = mirror[r][1] * scale
        space = lattice_transform(
            [(field_ref[k, 0, :, cut], field_ref[k, 1, :, cut]) for k in spot], 1
        )
        source = []
        for r in range(momenta):
            re, im = space[r]
            sq_re = re * re - im * im
            sq_im = 2.0 * re * im
            m_re, m_im = mirror_ref[r, 0, :, cut], mirror_ref[r, 1, :, cut]
            source.append((sq_re * m_re - sq_im * m_im, sq_re * m_im + sq_im * m_re))
        sigma = lattice_transform(source, -1)
        w = weights_ref[zl, :, cut]
        for q in range(momenta):
            sigma_ref[spot[q], 0, :, cut] = sigma[q][0] * w
            sigma_ref[spot[q], 1, :, cut] = sigma[q][1] * w


def self_energy(momentum_map, weights, field, mirror=None):
    first = mirror is None
    momenta, _, rows, cols = field.shape
    shape = jax.ShapeDtypeStruct((momenta, 2, rows, cols), jnp.float32)
    smem = pl.BlockSpec(memory_space=pltpu.SMEM)
    vmem = pl.BlockSpec(memory_space=pltpu.VMEM)
    ins = [momentum_map, weights, field] + ([] if first else [mirror])
    return pl.pallas_call(
        lambda *refs: self_energy_kernel(first, *refs),
        out_shape=(shape, shape) if first else shape,
        in_specs=[smem] + [vmem] * (len(ins) - 1),
        out_specs=(vmem, vmem) if first else vmem,
        scratch_shapes=[pltpu.SMEM((momenta,), jnp.int32)],
        compiler_params=pltpu.CompilerParams(vmem_limit_bytes=VMEM),
        name="self_energy_first" if first else "self_energy_next",
    )(*ins)


def split_left(x):
    hi = x.astype(jnp.bfloat16)
    lo = (x - hi.astype(jnp.float32)).astype(jnp.bfloat16)
    return jnp.concatenate([hi, lo, hi], axis=1)


def split_right(x):
    hi = x.astype(jnp.bfloat16)
    lo = (x - hi.astype(jnp.float32)).astype(jnp.bfloat16)
    return jnp.concatenate([hi, hi, lo], axis=0)


def mul(a, b):
    return jnp.dot(split_left(a), split_right(b), preferred_element_type=jnp.float32)


def product_kernel(counts, tiled, n_done, blocks_ref, *refs):
    terms = []
    for n in counts:
        terms.append((refs[:n], refs[n]))
        refs = refs[n + 1 :]
    base_ref, done, outs = refs[0], refs[1 : 1 + n_done], refs[1 + n_done :]

    def flat(x):
        return x.reshape(x.shape[0] * x.shape[1], x.shape[2])

    def left(holders, j):
        x = holders[0][:, j]
        for ref in holders[1:]:
            x = x + ref[:, j]
        return flat(x)

    re, im = base_ref[0], base_ref[1]
    for holders, panel_ref in terms:
        s_re, s_im = left(holders, 0), left(holders, 1)
        g_re, g_im = flat(panel_ref[:, 0]), flat(panel_ref[:, 1])
        one = mul(s_re, g_re)
        two = mul(s_im, g_im)
        three = mul(s_re + s_im, g_re + g_im)
        re, im = re + (one - two), im + (three - one - two)
    rows = re.shape[0]
    for i, pair in enumerate([(ref[0], ref[1]) for ref in done] + [(re, im)]):
        for j in range(2):
            outs[0][j, i * rows : (i + 1) * rows] = pair[j]
            if tiled:
                slabs = outs[1].shape[0] // (n_done + 1)
                outs[1][i * slabs : (i + 1) * slabs, j] = pair[j].reshape(
                    (slabs,) + outs[1].shape[2:]
                )


def product(terms, panel, base, chunk=0, done=(), tiled=False):
    slabs, _, high, cols = terms[0][0][0].shape
    rows = slabs * high
    per = cols // panel.shape[2]
    full = lambda shape: pl.BlockSpec(shape, lambda i, b: (0,) * len(shape))
    in_specs, ins = [], []
    for j, (lefts, _) in enumerate(terms):
        in_specs += [full(x.shape) for x in lefts]
        in_specs.append(
            pl.BlockSpec((per,) + panel.shape[1:], lambda i, b, j=j: (b[j], 0, 0, 0))
        )
        ins += list(lefts) + [panel]
    in_specs.append(pl.BlockSpec((2, rows, cols), lambda i, b: (0, chunk, 0)))
    in_specs += [full(x.shape) for x in done]
    outs = [jax.ShapeDtypeStruct((2, rows * (1 + len(done)), cols), jnp.float32)]
    if tiled:
        outs.append(jax.ShapeDtypeStruct((slabs * (1 + len(done)), 2, high, cols), jnp.float32))
    counts = [len(lefts) for lefts, _ in terms]
    return pl.pallas_call(
        lambda *refs: product_kernel(counts, tiled, len(done), *refs),
        out_shape=outs,
        grid_spec=pltpu.PrefetchScalarGridSpec(
            num_scalar_prefetch=1,
            grid=(1,),
            in_specs=in_specs,
            out_specs=[full(o.shape) for o in outs],
        ),
        compiler_params=pltpu.CompilerParams(vmem_limit_bytes=VMEM),
        name="product_last" if done else "product",
    )(jnp.stack([block for _, block in terms]), *ins, base, *done)


def time_product(sigma, panel, free, tiled):
    zl = lax.axis_index("zl")
    low = zl < 2
    near_block = lax.bitwise_xor(zl, 1)
    two_block, far_block = jnp.where(low, 2, 1), jnp.where(low, 3, 0)
    across, middle, outwards = [(0, 1), (1, 0), (2, 3), (3, 2)], [(1, 2), (2, 1)], [(1, 0), (2, 3)]

    def send(x, pairs):
        return lax.ppermute(x, "zl", pairs)

    mid = send(sigma, middle)
    near = send(sigma, across)
    end_two = send(mid, outwards)
    slabs = sigma.shape[0] // CHUNKS
    mid_far, end_far = [], []
    for i in range(CHUNKS):
        mid_far.append(send(near[i * slabs : (i + 1) * slabs], middle))
        end_far.append(send(mid_far[i], outwards))
    total = product([([sigma], zl), ([near], near_block)], panel, free)[0]
    total = product([([mid, end_two], two_block)], panel, total)[0]
    done = []
    for i in range(CHUNKS):
        last = i == CHUNKS - 1
        res = product(
            [([mid_far[i], end_far[i]], far_block)],
            panel,
            total,
            chunk=i,
            done=done if last else (),
            tiled=tiled and last,
        )
        done.append(res[0])
    return res


def pack(free, greater):
    return jnp.concatenate([free, greater], axis=0).swapaxes(0, 1)


def exchange(x):
    return lax.all_to_all(x, ("y", "zh"), 0, 0, tiled=True)


def body(g_free, g_greater_t, momentum_map, weights):
    momenta = momentum_map.shape[0]
    free, greater = g_free[:, 0], g_greater_t[:, 0]
    tile_rows, tile_cols = free.shape[1:]
    slabs = (2, momenta, tile_rows // momenta, tile_cols)
    weights = weights.reshape(-1, 1, tile_cols)

    green = free
    field = exchange(pack(free.reshape(slabs), greater.reshape(slabs)))
    mirror = None
    for sweep in range(ITERS):
        panel = lax.all_gather(green, ("x", "core"))
        panel = pltpu.with_memory_space_constraint(panel, pltpu.HBM)
        if mirror is None:
            sigma, mirror = self_energy(momentum_map, weights, field)
        else:
            sigma = self_energy(momentum_map, weights, field, mirror)
        sigma = exchange(sigma)
        if sweep == ITERS - 1:
            return time_product(sigma, panel, free, False)[0][:, None]
        green, tiles = time_product(sigma, panel, free, True)
        field = exchange(tiles)


def solution(mesh):
    fine = Mesh(mesh.devices.reshape(3, 8, 4, 4, 2), ("zh", "y", "zl", "x", "core"))
    spec = P(None, ("zh", "y"), ("x", "core"), "zl")
    return jax.shard_map(
        body, mesh=fine, in_specs=(spec, spec, P(), P()), out_specs=spec, check_vma=False
    )
```
